32 devices in a mesh: dp: 4 (over x, core), seq: 8 (over z, y).
Axes of the slice: x: 2, y: 2, z: 4, core: 2. Of those that a mesh axis runs over, the one named last changes fastest.
Arguments:
- q_raw: bfloat16 [4, 1024, 4096], P('dp', 'seq'), may hold values from -64 to 64
- k_raw: bfloat16 [4, 1024, 4096], P('dp', 'seq'), may hold values from -64 to 64
- values: bfloat16 [4, 1024, 4096], P('dp', 'seq'), may hold values from -6 to 6
- grad_out: bfloat16 [4, 1024, 4096], P('dp', 'seq'), may hold values from -6 to 6
- q_gain: float32 [4096], replicated, may hold values from 0.1 to 1.9
- k_gain: float32 [4096], replicated, may hold values from 0.1 to 1.9
- lengths: int32 [4, 6], P('dp'), may hold values from 1 to 341, 1024 in all within a row
- positions: int32 [4, 3, 1024], P('dp', None, 'seq'), may hold values from 0 to 63
Outputs:
- attended: bfloat16 [4, 1024, 4096], P('dp', 'seq')
- grad_q: bfloat16 [4, 1024, 4096], P('dp', 'seq')
- grad_k: bfloat16 [4, 1024, 4096], P('dp', 'seq')
- grad_v: bfloat16 [4, 1024, 4096], P('dp', 'seq')
- grad_q_gain: float32 [4096], replicated
- grad_k_gain: float32 [4096], replicated
The draws below stay inside these ranges and needn't reach their ends.
Inputs may be any that keep to these rules, and one draw needn't show every extreme that they name: `lengths`: the clips of a bucket lie end to end and fill its 1024 tokens.
All inputs are finite; a program needn't handle non-finite values.
Results may differ from the reference program's by a relative error of at most 0.012.
The reference program's roundings to bfloat16 on the way (of `weights`, `prob_half` and `dscore`) count: a program that leaves them out, or rounds other values in their place, can miss the bound.
Values may be sent and summed in bfloat16 or wider, within the bound.
A program may use at most 128 MiB of HBM per device.

```python
import math
import jax
import jax.numpy as jnp
import numpy as np
from jax import lax

HEADS = 32
HEAD_DIM = 128
FEAT = 4096
TOKENS = 1024
CLIPS = 6
CLIP_MOST = 341
GRID = 64
N_DP = 4


def draw_pair(key):
    base = jax.random.fold_in(key, 11)
    shape = (N_DP, TOKENS, FEAT)
    query = jax.random.normal(jax.random.fold_in(base, 1), shape, jnp.float32)
    keys = jax.random.normal(jax.random.fold_in(base, 2), shape, jnp.float32)
    return (jnp.clip(query, -64.0, 64.0), jnp.clip(keys, -64.0, 64.0))


def draw_q_raw(key, part):
    return draw_pair(key)[0].astype(jnp.bfloat16)


def draw_k_raw(key, part):
    return draw_pair(key)[1].astype(jnp.bfloat16)


def plant(array, rng, least, top_value):
    place = [jax.random.randint(jax.random.fold_in(rng, axis), (), 0, length) for axis, length in enumerate(array.shape)]
    main_axis = array.shape.index(max(array.shape))
    beside = place[:main_axis] + [(place[main_axis] + 1) % array.shape[main_axis]] + place[main_axis + 1:]
    return array.at[tuple(place)].set(least).at[tuple(beside)].set(top_value)


def block_scale(rng, extent, pieces, least, top_value):
    factor_of, own = 1.0, jax.random.fold_in(rng, 6)
    for axis_at, parts in pieces:
        draws = jnp.exp(jax.random.uniform(jax.random.fold_in(own, axis_at), (parts,), jnp.float32, least / len(pieces), top_value / len(pieces)))
        factor_of = factor_of * jnp.repeat(draws, extent[axis_at] // parts).reshape([-1 if axis == axis_at else 1 for axis in range(len(extent))])
    return factor_of


def length_profile(amount, total, most, skew):
    weights = [(1 << 20) // math.isqrt(standing ** skew) + 1 for standing in range(2, amount + 1)]
    surplus, counts = total - most - (amount - 1), [1] * (amount - 1)
    while surplus > 0:
        free = [i for i in range(amount - 1) if counts[i] < most]
        pool, budget = sum([weights[i] for i in free]), surplus
        for i in free:
            extra = min(most - counts[i], max(1, budget * weights[i] // pool), surplus)
            counts[i] = counts[i] + extra
            surplus = surplus - extra
    return np.array([most] + counts)


def ragged(rng, number_of, total, most, skew):
    if number_of == 2:
        one = jax.random.randint(rng, (), max(1, total - most), min(most, total - 1) + 1)
        return jnp.stack([one, total - one])
    sizes = jnp.asarray(length_profile(number_of, total, most, skew), jnp.int32)
    pairs = (number_of - 1) // 2
    source_of, sink = sizes[1:1 + 2 * pairs:2], sizes[2:2 + 2 * pairs:2]
    slack = jnp.minimum(source_of - 1, most - sink)
    moved = jax.random.randint(jax.random.fold_in(rng, 1), (pairs,), 0, 1 << 20) % (slack + 1)
    sizes = sizes.at[1:1 + 2 * pairs:2].set(source_of - moved).at[2:2 + 2 * pairs:2].set(sink + moved)
    return sizes[jax.random.permutation(jax.random.fold_in(rng, 2), number_of)]


def noise(own_key, shape, scale, limit, shards=(), held_as=jnp.bfloat16):
    factor_of = block_scale(own_key, shape, shards, -0.22, 0.18) if shards else 1.0
    entries = jax.random.normal(own_key, shape, jnp.float32) * scale * factor_of
    return jnp.minimum(jnp.maximum(entries, -limit), limit).astype(held_as)


def setup_inputs(seed: int = 0) -> dict:
    arg_keys = jax.random.split(jax.random.key(seed), 9)
    q_raw = draw_q_raw(jax.random.fold_in(arg_keys[8], 71), 0)
    k_raw = draw_k_raw(jax.random.fold_in(arg_keys[8], 71), 0)
    values = noise(arg_keys[2], (N_DP, TOKENS, FEAT), 1.0, 6.0, ((0, 4), (1, 8)))
    grad_out = noise(arg_keys[3], (N_DP, TOKENS, FEAT), 1.0, 6.0, ((0, 4), (1, 8)))
    q_gain = jnp.clip(1.0 + 0.18 * jax.random.normal(arg_keys[4], (FEAT,), jnp.float32), 0.1, 1.9)
    k_gain = jnp.clip(1.0 + 0.18 * jax.random.normal(arg_keys[5], (FEAT,), jnp.float32), 0.1, 1.9)
    lengths = jax.vmap(lambda own: ragged(own, CLIPS, TOKENS, CLIP_MOST, 2))(jax.random.split(arg_keys[6], N_DP)).reshape((N_DP, CLIPS)).astype(jnp.int32)
    positions = plant(jax.random.randint(arg_keys[7], (N_DP, 3, TOKENS), 0, GRID), jax.random.fold_in(arg_keys[7], 1), 0, GRID - 1).astype(jnp.int32)
    return {"q_raw": q_raw, "k_raw": k_raw, "values": values, "grad_out": grad_out, "q_gain": q_gain, "k_gain": k_gain, "lengths": lengths, "positions": positions}


epsilon = 1e-06

def product(form, left, right):
    return jnp.einsum(form, left.astype(jnp.float32), right.astype(jnp.float32))

def segment_ids(clip_lengths, tokens):
    boundary = jnp.cumsum(clip_lengths).astype(jnp.int32)
    places = jnp.arange(tokens, dtype=jnp.int32)
    return lax.optimization_barrier(jnp.sum((boundary[None, :] <= places[:, None]).astype(jnp.int32), axis=1)).astype(jnp.int32)

def rope_tables(position_rows, head_dim):
    half = head_dim // 2
    sixth = head_dim // 6
    first = half - 2 * sixth
    pairs = jnp.arange(half, dtype=jnp.int32)
    section = (pairs >= first).astype(jnp.int32) + (pairs >= first + sixth).astype(jnp.int32)
    begin = jnp.where(section == 0, 0, jnp.where(section == 1, first, first + sixth))
    number = jnp.where(section == 0, first, sixth)
    freqs = 10000.0 ** (-(pairs - begin).astype(jnp.float32) / number.astype(jnp.float32))
    picker = (section[None, :] == jnp.arange(3, dtype=jnp.int32)[:, None]).astype(jnp.float32) * freqs[None, :]
    angle = lax.dot_general(position_rows.astype(jnp.float32), picker, (((0,), (0,)), ((), ())), precision=lax.Precision.HIGHEST)
    cosine = jnp.cos(angle)
    sine = jnp.sin(angle)
    return (jnp.concatenate([cosine, cosine], axis=-1), jnp.concatenate([sine, sine], axis=-1))

def rotate_pairs(inputs, cosine, sine):
    half = inputs.shape[-1] // 2
    partner = jnp.concatenate([-inputs[..., half:], inputs[..., :half]], axis=-1)
    return inputs * cosine[:, None, :] + partner * sine[:, None, :]

def rotate_back(grads, cosine, sine):
    half = grads.shape[-1] // 2
    turned = grads * sine[:, None, :]
    return grads * cosine[:, None, :] + jnp.concatenate([turned[..., half:], -turned[..., :half]], axis=-1)

def attention_forward(query, keys, value_rows, segment, block, window, reach):
    count = query.shape[0]
    scale = query.shape[2] ** (-0.5)

    def one_block(index_block):
        start = (index_block * block).astype(jnp.int32)
        key_start = jnp.clip(start - reach, 0, count - window).astype(jnp.int32)
        query_block = lax.dynamic_slice_in_dim(query, start, block, 0)
        key_window = lax.dynamic_slice_in_dim(keys, key_start, window, 0)
        value_window = lax.dynamic_slice_in_dim(value_rows, key_start, window, 0)
        query_clip = lax.dynamic_slice_in_dim(segment, start, block, 0)
        key_clip = lax.dynamic_slice_in_dim(segment, key_start, window, 0)
        scores = product('qhd,khd->hqk', query_block, key_window) * scale
        live = (query_clip[:, None] == key_clip[None, :])[None]
        scores = jnp.where(live, scores, -1e+30)
        highest = lax.optimization_barrier(jnp.max(scores, axis=-1, keepdims=True))
        expon = jnp.exp(scores - highest)
        totals = lax.optimization_barrier(jnp.sum(expon, axis=-1, keepdims=True))
        weights = (expon / totals).astype(jnp.bfloat16)
        output = product('hqk,khd->qhd', weights, value_window)
        return (output, (highest + jnp.log(totals))[..., 0])
    outputs, logsum = lax.map(one_block, jnp.arange(count // block, dtype=jnp.int32))
    return (outputs.reshape(query.shape), logsum)

def attention_backward(query, keys, value_rows, context, cotangent, logsum, segment, block, window, reach):
    count = query.shape[0]
    scale = query.shape[2] ** (-0.5)
    delta = lax.optimization_barrier(jnp.sum(cotangent.astype(jnp.float32) * context.astype(jnp.float32), axis=-1))

    def one_block(carry, inputs):
        key_acc, value_acc = carry
        index_block, block_logsum = inputs
        start = (index_block * block).astype(jnp.int32)
        key_start = jnp.clip(start - reach, 0, count - window).astype(jnp.int32)
        query_block = lax.dynamic_slice_in_dim(query, start, block, 0)
        cot_block = lax.dynamic_slice_in_dim(cotangent, start, block, 0)
        delta_block = lax.dynamic_slice_in_dim(delta, start, block, 0)
        key_window = lax.dynamic_slice_in_dim(keys, key_start, window, 0)
        value_window = lax.dynamic_slice_in_dim(value_rows, key_start, window, 0)
        query_clip = lax.dynamic_slice_in_dim(segment, start, block, 0)
        key_clip = lax.dynamic_slice_in_dim(segment, key_start, window, 0)
        scores = product('qhd,khd->hqk', query_block, key_window) * scale
        live = (query_clip[:, None] == key_clip[None, :])[None]
        probs = jnp.where(live, jnp.exp(scores - block_logsum[:, :, None]), 0.0)
        prob_half = probs.astype(jnp.bfloat16)
        value_grad = product('hqk,qhd->khd', prob_half, cot_block)
        dprob = product('qhd,khd->hqk', cot_block, value_window)
        dscore = (probs * (dprob - jnp.transpose(delta_block)[:, :, None]) * scale).astype(jnp.bfloat16)
        query_grad = product('hqk,khd->qhd', dscore, key_window)
        key_grad = product('hqk,qhd->khd', dscore, query_block)
        key_acc = lax.dynamic_update_slice_in_dim(key_acc, lax.dynamic_slice_in_dim(key_acc, key_start, window, 0) + key_grad, key_start, 0)
        value_acc = lax.dynamic_update_slice_in_dim(value_acc, lax.dynamic_slice_in_dim(value_acc, key_start, window, 0) + value_grad, key_start, 0)
        return ((key_acc, value_acc), query_grad)
    zeros = jnp.zeros(query.shape, jnp.float32)
    indices = jnp.arange(count // block, dtype=jnp.int32)
    (key_acc, value_acc), query_grads = lax.scan(one_block, (zeros, zeros), (indices, logsum))
    return (query_grads.reshape(query.shape), key_acc, value_acc)

def norm_backward(grads_half, cosine, sine, scale_rows, hat_rows, gain_row):
    tokens = hat_rows.shape[0]
    grads = lax.optimization_barrier(grads_half).astype(jnp.float32)
    turned = rotate_back(grads, cosine, sine).reshape(tokens, -1)
    gain_part = lax.optimization_barrier(jnp.sum(turned * hat_rows, axis=0))
    lifted = turned * gain_row
    inner = lax.optimization_barrier(jnp.mean(lifted * hat_rows, axis=-1, keepdims=True))
    return ((scale_rows[:, None] * (lifted - hat_rows * inner)).astype(jnp.bfloat16), gain_part)

def reference(q_raw, k_raw, values, grad_out, q_gain, k_gain, lengths, positions):
    reach = CLIP_MOST
    block = min(512, TOKENS)
    window = min(TOKENS, block + 2 * reach)

    def replica(inputs):
        query_raw, key_raw, value_rows, cot_rows, clip_lengths, position_rows = inputs
        segment = segment_ids(clip_lengths, TOKENS)
        cosine, sine = rope_tables(position_rows, HEAD_DIM)
        query_float = query_raw.astype(jnp.float32)
        key_float = key_raw.astype(jnp.float32)
        query_scale = lax.rsqrt(lax.optimization_barrier(jnp.mean(query_float * query_float, axis=-1)) + epsilon)
        key_scale = lax.rsqrt(lax.optimization_barrier(jnp.mean(key_float * key_float, axis=-1)) + epsilon)
        query_hat = query_float * query_scale[:, None]
        key_hat = key_float * key_scale[:, None]
        query_rot = rotate_pairs((query_hat * q_gain).reshape(TOKENS, HEADS, HEAD_DIM), cosine, sine).astype(jnp.bfloat16)
        key_rot = rotate_pairs((key_hat * k_gain).reshape(TOKENS, HEADS, HEAD_DIM), cosine, sine).astype(jnp.bfloat16)
        value_heads = value_rows.reshape(TOKENS, HEADS, HEAD_DIM)
        context, logsum = attention_forward(query_rot, key_rot, value_heads, segment, block, window, reach)
        context_half = context.astype(jnp.bfloat16)
        cot_heads = cot_rows.reshape(TOKENS, HEADS, HEAD_DIM)
        query_grad, key_grad, value_grad = attention_backward(query_rot, key_rot, value_heads, context_half, cot_heads, logsum, segment, block, window, reach)
        query_input, query_part = norm_backward(query_grad.astype(jnp.bfloat16), cosine, sine, query_scale, query_hat, q_gain)
        key_input, key_part = norm_backward(key_grad.astype(jnp.bfloat16), cosine, sine, key_scale, key_hat, k_gain)
        return (context_half.reshape(TOKENS, FEAT), query_input, key_input, value_grad.astype(jnp.bfloat16).reshape(TOKENS, FEAT), query_part, key_part)
    attended, grad_q, grad_k, grad_v, query_parts, key_parts = lax.map(replica, (q_raw, k_raw, values, grad_out, lengths, positions))
    return (attended, grad_q, grad_k, grad_v, lax.optimization_barrier(jnp.sum(query_parts, axis=0)) / N_DP, lax.optimization_barrier(jnp.sum(key_parts, axis=0)) / N_DP)
```

```python
import functools

import jax
import jax.numpy as jnp
import numpy as np
from jax import lax
from jax.experimental import pallas as pl
from jax.experimental.pallas import tpu as pltpu
from jax.sharding import PartitionSpec as P

HEAD_DIM = 128
LANES = 128
QUERY_BLOCK = 256
GROUPS = 4
CHUNK = 2
TILE = 16
ATTEND_LAG = 2
DISTRIBUTE_LAG = 1
EPSILON = 1e-06
MESH = pl.DeviceIdType.MESH


def rope_tables(position_rows, head_dim):
    half = head_dim // 2
    sixth = head_dim // 6
    first = half - 2 * sixth
    pairs = np.arange(head_dim) % half
    section = (pairs >= first).astype(np.int32) + (pairs >= first + sixth).astype(np.int32)
    begin = np.where(section == 0, 0, np.where(section == 1, first, first + sixth))
    number = np.where(section == 0, first, sixth)
    freqs = (10000.0 ** (-(pairs - begin) / number)).astype(np.float32)
    sign = np.where(np.arange(head_dim) < half, -1.0, 1.0).astype(np.float32)
    rows = position_rows.astype(jnp.float32)[:, :, None]
    chosen = jnp.where(section == 0, rows[0], jnp.where(section == 1, rows[1], rows[2]))
    angle = chosen * freqs
    return jnp.cos(angle), jnp.sin(angle) * sign


def slot_sizes(longest, group_tokens, chunk):
    capacity = TILE
    while True:
        sizes = {n: min(group_tokens, capacity // n // TILE * TILE) for n in range(1, chunk + 1)}

        def fits(below, above):
            return any(
                (n == 0 or below <= sizes[n]) and (n == chunk or above <= sizes[chunk - n])
                for n in range(chunk + 1)
            )

        spill = longest - group_tokens - 1
        if spill <= sizes[chunk] and all(fits(a, longest - a) for a in range(1, longest)):
            return capacity, sizes
        capacity += TILE


def dot(left, right, left_dim, right_dim):
    return lax.dot_general(
        left, right, (((left_dim,), (right_dim,)), ((), ())), preferred_element_type=jnp.float32
    )


def kernel(
    sizes,
    len_ref, q_ref, k_ref, v_ref, do_ref, gq_ref, gk_ref, cos_ref, sin_ref,
    out_ref, gain_ref,
    give, take, give_back, take_back, sent, recv, back, key_acc, value_acc, scale_q, scale_k,
    part, seq_part, dp_sum, dp_part, total,
    in_send, in_recv, own_sem, out_send, out_recv, gain_send, gain_recv,
    halo_send, halo_recv, beside_send, beside_recv,
):
    n, replicas, heads, tok, clips, reach, capacity, slots, window, padded = sizes
    members = n // GROUPS
    group_tokens = members * tok
    chunks = heads // CHUNK
    low = [slots[index + 1] for index in range(CHUNK)]
    own_end = [below + group_tokens for below in low]
    feature = members * heads * HEAD_DIM
    ratio = GROUPS
    shared = heads // ratio
    me = lax.axis_index("seq")
    side = me // members
    place_in = lax.rem(me, members)
    my_dp = lax.axis_index("dp")
    scale = HEAD_DIM ** (-0.5)

    def peer(step):
        return lax.rem(me + step, n)

    def member(step):
        return lax.rem(place_in + step, members)

    def device(group, index):
        return (my_dp, group * members + index)

    def columns(owner, head):
        return pl.ds(pl.multiple_of((owner * heads + head) * HEAD_DIM, HEAD_DIM), HEAD_DIM)

    def rows(owner, index):
        return pl.ds(pl.multiple_of(low[index] + owner * tok, TILE), tok)

    def each_side(act):
        @pl.when(side > 0)
        def _():
            act(0, side - 1)

        @pl.when(side < GROUPS - 1)
        def _():
            act(1, side + 1)

    def remote(src, dst, send_sem, recv_sem, device):
        return pltpu.make_async_remote_copy(
            src_ref=src, dst_ref=dst, send_sem=send_sem, recv_sem=recv_sem,
            device_id=device, device_id_type=MESH,
        )

    barrier = pltpu.get_barrier_semaphore()
    for step in range(1, n):
        pl.semaphore_signal(barrier, inc=1, device_id=(my_dp, peer(step)), device_id_type=MESH)
    for step in range(1, replicas):
        other = lax.rem(my_dp + step, replicas)
        pl.semaphore_signal(barrier, inc=1, device_id=(other, me), device_id_type=MESH)
    pl.semaphore_wait(barrier, n - 1 + replicas - 1)

    def send_values(head, index):
        cols = columns(place_in, head)
        for place, ref in ((2, v_ref), (3, do_ref)):
            pltpu.make_async_copy(
                ref.at[:, cols], recv.at[head, place, rows(place_in, index), :], own_sem.at[head]
            ).start()

        @pl.loop(1, members)
        def _(step):
            other = member(step)
            for place, ref in ((2, v_ref), (3, do_ref)):
                remote(
                    ref.at[:, columns(other, head)], recv.at[head, place, rows(place_in, index), :],
                    in_send.at[head], in_recv.at[head], device(side, other),
                ).start()

    for index in range(CHUNK):
        send_values(index, index)

    def squares(index, sums):
        cols = pl.ds(pl.multiple_of(index * LANES, LANES), LANES)
        query = q_ref[:, cols].astype(jnp.float32)
        keys = k_ref[:, cols].astype(jnp.float32)
        return sums[0] + query * query, sums[1] + keys * keys

    zero = jnp.zeros((tok, LANES), jnp.float32)
    sum_q, sum_k = lax.fori_loop(0, feature // LANES, squares, (zero, zero))
    for sums, target in ((sum_q, scale_q), (sum_k, scale_k)):
        mean = jnp.sum(sums, axis=1, keepdims=True) / feature
        target[...] = jnp.broadcast_to(lax.rsqrt(mean + EPSILON), (tok, LANES))

    def rotated(ref, gain, norm, cols):
        x = ref[:, cols].astype(jnp.float32) * norm[...] * gain[:, cols]
        turned = x * cos_ref[...] + pltpu.roll(x, HEAD_DIM // 2, 1) * sin_ref[...]
        return turned.astype(jnp.bfloat16)

    @pl.loop(0, chunks)
    def _(chunk):
        @pl.when(chunk > 0)
        def _():
            for index in range(CHUNK):
                send_values(chunk * CHUNK + index, index)

        for index in range(CHUNK):
            head = chunk * CHUNK + index

            @pl.loop(1, members)
            def _(step):
                other = member(step)
                cols = columns(other, head)
                sent[head, other, 0] = rotated(q_ref, gq_ref, scale_q, cols)
                sent[head, other, 1] = rotated(k_ref, gk_ref, scale_k, cols)
                remote(
                    sent.at[head, other], recv.at[head, 0:2, rows(place_in, index), :],
                    in_send.at[head], in_recv.at[head], device(side, other),
                ).start()

            cols = columns(place_in, head)
            for place, (ref, gain, norm) in enumerate(
                ((q_ref, gq_ref, scale_q), (k_ref, gk_ref, scale_k))
            ):
                recv[head, place, rows(place_in, index), :] = rotated(ref, gain, norm, cols)

    bounds = []
    running = len_ref[0, 0]
    for clip in range(clips):
        bounds.append(running)
        if clip + 1 < clips:
            running = running + len_ref[0, clip + 1]

    def straddle(middle):
        first, last = jnp.int32(0), jnp.int32(n * tok)
        for bound in bounds:
            first = jnp.maximum(first, jnp.where(bound <= middle, bound, 0))
            last = jnp.minimum(last, jnp.where(bound > middle, bound, n * tok))
        below, above = middle - first, last - middle
        mode = jnp.int32(0)
        for count in range(1, CHUNK + 1):
            fits = below <= slots[count]
            if count < CHUNK:
                fits = fits & (above <= slots[CHUNK - count])
            mode = jnp.where(fits, count, mode)
        return first, last, mode

    token_start = side * group_tokens
    straddles = straddle(token_start), straddle(token_start + group_tokens)

    def clear(index, begin, end):
        @pl.loop(0, chunks)
        def _(chunk):
            recv[chunk * CHUNK + index, :, begin:end, :] = jnp.zeros(
                (4, end - begin, HEAD_DIM), jnp.bfloat16
            )

    for index in range(CHUNK):
        above = own_end[index] + slots[CHUNK - index]
        if padded > above:
            clear(index, above, padded)

        @pl.when(side == 0)
        def _():
            clear(index, 0, low[index])

        @pl.when(side == GROUPS - 1)
        def _():
            clear(index, own_end[index], above)

    def segment(shape, dim, start, shift):
        inside = lax.broadcasted_iota(jnp.int32, shape, dim) + start
        places = inside + (token_start - shift)
        found = jnp.zeros(shape, jnp.int32)
        for bound in bounds:
            found = found + (places >= bound).astype(jnp.int32)
        valid = (inside < window) & (places >= 0) & (places < n * tok)
        return jnp.where(valid, found, -1)

    def taken(upward):
        table = []
        for mode in range(CHUNK + 1):
            if upward:
                size = slots[mode] if mode else 0
                table.append([(index, index * size, size) for index in range(mode)])
            else:
                size = slots[CHUNK - mode] if mode < CHUNK else 0
                table.append([(index, (index - mode) * size, size) for index in range(mode, CHUNK)])
        return table

    def place_of(upward, halo, index, size):
        if upward:
            return (low[index] if halo else own_end[index]) - size
        return own_end[index] if halo else low[index]

    def modes(which):
        held = jnp.full((TILE, HEAD_DIM), straddles[which][2], jnp.int32)
        return [held == mode for mode in range(CHUNK + 1)]

    def gather(target, source, which, upward, halo, chunk):
        masks = modes(which)

        @pl.loop(0, 4)
        def _(place):
            for begin in range(0, capacity, TILE):
                value = None
                for mode, table in enumerate(taken(upward)):
                    for index, start, size in table:
                        if start <= begin < start + size:
                            row = place_of(upward, halo, index, size) + begin - start
                            found = source[chunk * CHUNK + index, place, row:row + TILE, :]
                            value = found if value is None else jnp.where(masks[mode], found, value)
                if value is None:
                    value = jnp.zeros((TILE, HEAD_DIM), jnp.bfloat16)
                target[chunk, which, place, begin:begin + TILE, :] = value

    def scatter(source, target, which, upward, halo, chunk):
        masks = modes(which)
        first, last, mode_now = straddles[which]
        lane_rows = lax.broadcasted_iota(jnp.int32, (TILE, HEAD_DIM), 0)
        limits = []
        for mode in range(CHUNK + 1):
            if upward:
                limits.append(jnp.where(mode_now == mode, first, n * tok))
            else:
                limits.append(jnp.where(mode_now == mode, last, -1))

        @pl.loop(0, 4)
        def _(place):
            for index in range(CHUNK):
                span = slots[index + 1] if upward else slots[CHUNK - index]
                base = place_of(upward, halo, index, span)
                for row in range(base, base + span, TILE):
                    value = None if halo else target[chunk * CHUNK + index, place, row:row + TILE, :]
                    tokens = lane_rows + (token_start + row - low[index])
                    for mode, table in enumerate(taken(upward)):
                        for owner, start, size in table:
                            begin = place_of(upward, halo, owner, size)
                            if owner == index and begin <= row < begin + size:
                                offset = start + row - begin
                                found = source[chunk, which, place, offset:offset + TILE, :]
                                if halo:
                                    mask = masks[mode]
                                elif upward:
                                    mask = tokens >= limits[mode]
                                else:
                                    mask = tokens < limits[mode]
                                value = found if value is None else jnp.where(mask, found, value)
                    target[chunk * CHUNK + index, place, row:row + TILE, :] = value

    def relay(chunk):
        for index in range(CHUNK):
            head = chunk * CHUNK + index
            arrived = recv.at[head, :, pl.ds(0, (members - 1) * tok), :]
            pltpu.make_async_copy(arrived, arrived, in_recv.at[head]).wait()
            own = recv.at[head, pl.ds(2, 2), pl.ds(0, tok), :]
            pltpu.make_async_copy(own, own, own_sem.at[head]).wait()

        def act(which, group):
            gather(give, recv, which, which == 1, False, chunk)
            remote(
                give.at[chunk, which], take.at[chunk, 1 - which],
                halo_send.at[which, chunk], halo_recv.at[1 - which, chunk], device(group, place_in),
            ).start()

        each_side(act)

    def attend(chunk):
        def arrive(which, group):
            held = take.at[chunk, which]
            pltpu.make_async_copy(held, held, halo_recv.at[which, chunk]).wait()
            scatter(take, recv, which, which == 0, True, chunk)

        each_side(arrive)

        @pl.loop(0, CHUNK)
        def _(index):
            shift = jnp.int32(low[0])
            for other in range(1, CHUNK):
                shift = jnp.where(index == other, low[other], shift)
            attend_head(chunk * CHUNK + index, shift)

        def act(which, group):
            gather(give_back, back, which, which == 0, True, chunk)
            remote(
                give_back.at[chunk, which], take_back.at[chunk, 1 - which],
                beside_send.at[which, chunk], beside_recv.at[1 - which, chunk],
                device(group, place_in),
            ).start()

        each_side(act)

    def attend_head(head, shift):
        key_acc[...] = jnp.zeros_like(key_acc)
        value_acc[...] = jnp.zeros_like(value_acc)
        for start in range(0, window, QUERY_BLOCK):
            block = min(QUERY_BLOCK, window - start)
            first = max(0, start - reach) // LANES * LANES
            last = min(padded, -(-(start + block + reach) // LANES) * LANES)
            query = recv[head, 0, start:start + block, :]
            keys = recv[head, 1, first:last, :]
            value_rows = recv[head, 2, first:last, :]
            cot = recv[head, 3, start:start + block, :]
            live = segment((block, 1), 0, start, shift) == segment((1, last - first), 1, first, shift)
            scores = jnp.where(live, dot(query, keys, 1, 1), -1e30)
            highest = jnp.max(scores, axis=1, keepdims=True)
            expon = jnp.exp((scores - highest) * scale)
            probs = expon * (1.0 / jnp.sum(expon, axis=1, keepdims=True))
            half = probs.astype(jnp.bfloat16)
            context = dot(half, value_rows, 1, 0).astype(jnp.bfloat16)
            delta = jnp.sum(
                cot.astype(jnp.float32) * context.astype(jnp.float32), axis=1, keepdims=True
            )
            dprob = dot(cot, value_rows, 1, 1)
            dscore = (probs * (dprob - delta) * scale).astype(jnp.bfloat16)
            back[head, 0, start:start + block, :] = context
            back[head, 1, start:start + block, :] = dot(dscore, keys, 1, 0).astype(jnp.bfloat16)
            key_acc[first:last, :] += dot(dscore, query, 0, 0)
            value_acc[first:last, :] += dot(half, cot, 0, 0)
        back[head, 2] = key_acc[0:window, :].astype(jnp.bfloat16)
        back[head, 3] = value_acc[0:window, :].astype(jnp.bfloat16)

    def distribute(chunk):
        def merge(which, group):
            held = take_back.at[chunk, which]
            pltpu.make_async_copy(held, held, beside_recv.at[which, chunk]).wait()
            scatter(take_back, back, which, which == 1, False, chunk)

        each_side(merge)
        for index in range(CHUNK):
            head = chunk * CHUNK + index
            cols = columns(place_in, head)

            @pl.loop(1, members)
            def _(step):
                other = member(step)
                remote(
                    back.at[head, :, rows(other, index), :], out_ref.at[:, :, cols],
                    out_send.at[head], out_recv.at[head], device(side, other),
                ).start()

            out_ref[:, :, cols] = back[head, :, rows(place_in, index), :]

    @pl.loop(0, chunks + ATTEND_LAG + DISTRIBUTE_LAG)
    def _(step):
        @pl.when(step < chunks)
        def _():
            relay(step)

        @pl.when((step >= ATTEND_LAG) & (step < chunks + ATTEND_LAG))
        def _():
            attend(step - ATTEND_LAG)

        @pl.when(step >= ATTEND_LAG + DISTRIBUTE_LAG)
        def _():
            distribute(step - ATTEND_LAG - DISTRIBUTE_LAG)

    def turned_back(place, ref, norm, cols):
        grads = out_ref[place, :, cols].astype(jnp.float32)
        turned = grads * cos_ref[...] - pltpu.roll(grads, HEAD_DIM // 2, 1) * sin_ref[...]
        return turned, ref[:, cols].astype(jnp.float32) * norm[...]

    inner = (zero, zero)
    for head in range(heads):
        arrived = out_ref.at[:, :, pl.ds(0, (members - 1) * HEAD_DIM)]
        pltpu.make_async_copy(arrived, arrived, out_recv.at[head]).wait()

        def first_pass(owner, sums):
            cols = columns(owner, head)
            results = []
            for place, (ref, gain, norm) in enumerate(
                ((q_ref, gq_ref, scale_q), (k_ref, gk_ref, scale_k))
            ):
                turned, hat = turned_back(place + 1, ref, norm, cols)
                both = turned * hat
                row = place * shared + head % shared
                part[owner * ratio + head // shared, row:row + 1, :] = jnp.sum(both, axis=0, keepdims=True)
                results.append(sums[place] + both * gain[:, cols])
            return tuple(results)

        inner = lax.fori_loop(0, members, first_pass, inner)

    @pl.loop(1, n)
    def _(step):
        other = peer(step)
        remote(
            part.at[other], seq_part.at[me], gain_send.at[0], gain_recv.at[0], (my_dp, other)
        ).start()

    seq_part[me] = part[me]
    inner_q, inner_k = (
        jnp.broadcast_to(jnp.sum(sums, axis=1, keepdims=True) / feature, (tok, LANES))
        for sums in inner
    )

    def second_pass(index):
        cols = pl.ds(pl.multiple_of(index * LANES, LANES), LANES)
        for place, (ref, gain, norm, mean) in enumerate(
            ((q_ref, gq_ref, scale_q, inner_q), (k_ref, gk_ref, scale_k, inner_k))
        ):
            turned, hat = turned_back(place + 1, ref, norm, cols)
            result = norm[...] * (turned * gain[:, cols] - hat * mean)
            out_ref[place + 1, :, cols] = result.astype(jnp.bfloat16)

    pl.loop(0, feature // LANES)(second_pass)

    def wait_all(ref, count, sem):
        held = ref.at[pl.ds(0, count)]
        pltpu.make_async_copy(held, held, sem).wait()

    wait_all(seq_part, n - 1, gain_recv.at[0])
    dp_sum[...] = jnp.sum(seq_part[...], axis=0)
    for step in range(1, replicas):
        other = lax.rem(my_dp + step, replicas)
        remote(
            dp_sum, dp_part.at[my_dp], gain_send.at[1], gain_recv.at[1], (other, me)
        ).start()
    dp_part[my_dp] = dp_sum[...]
    wait_all(dp_part, replicas - 1, gain_recv.at[1])
    total[...] = jnp.sum(dp_part[...], axis=0) / replicas

    @pl.loop(1, n)
    def _(step):
        other = peer(step)
        remote(
            total, gain_ref.at[me], gain_send.at[2], gain_recv.at[2], (my_dp, other)
        ).start()

    gain_ref[me] = total[...]
    wait_all(gain_ref, n - 1, gain_recv.at[2])

    wait_all(seq_part, n - 1, gain_send.at[0])
    wait_all(dp_part, replicas - 1, gain_send.at[1])
    wait_all(seq_part, n - 1, gain_send.at[2])
    for head in range(heads):
        moved = recv.at[head, :, pl.ds(0, (members - 1) * tok), :]
        pltpu.make_async_copy(moved, moved, in_send.at[head]).wait()
        pltpu.make_async_copy(moved, moved, out_send.at[head]).wait()

    @pl.loop(0, chunks)
    def _(chunk):
        def drain(which, group):
            held = give.at[chunk, which]
            pltpu.make_async_copy(held, held, halo_send.at[which, chunk]).wait()
            pltpu.make_async_copy(held, held, beside_send.at[which, chunk]).wait()

        each_side(drain)


def on_device(q_raw, k_raw, values, grad_out, q_gain, k_gain, lengths, positions):
    n = lax.axis_size("seq")
    replicas = lax.axis_size("dp")
    tok, feature = q_raw.shape[1:]
    shared = feature // n // HEAD_DIM
    heads = GROUPS * shared
    tokens = n * tok
    reach = tokens // 3 - 1
    group_tokens = tokens // GROUPS
    chunks = heads // CHUNK
    capacity, slots = slot_sizes(reach + 1, group_tokens, CHUNK)
    window = group_tokens + max(slots[i + 1] + slots[CHUNK - i] for i in range(CHUNK))
    padded = -(-window // LANES) * LANES
    cosine, sine = rope_tables(positions[0], HEAD_DIM)
    sizes = (n, replicas, heads, tok, lengths.shape[1], reach, capacity, slots, window, padded)
    vmem = pl.BlockSpec(memory_space=pltpu.VMEM)
    hbm = pl.BlockSpec(memory_space=pl.ANY)
    gain_rows = (2 * shared, LANES)
    half, full = jnp.bfloat16, jnp.float32
    outs, gains = pl.pallas_call(
        functools.partial(kernel, sizes),
        out_shape=(
            jax.ShapeDtypeStruct((4, tok, feature), half),
            jax.ShapeDtypeStruct((n,) + gain_rows, full),
        ),
        in_specs=[
            pl.BlockSpec(memory_space=pltpu.SMEM), vmem, vmem, hbm, hbm, vmem, vmem, vmem, vmem,
        ],
        out_specs=(vmem, vmem),
        scratch_shapes=[
            pltpu.VMEM((chunks, 2, 4, capacity, HEAD_DIM), half),
            pltpu.VMEM((chunks, 2, 4, capacity, HEAD_DIM), half),
            pltpu.VMEM((chunks, 2, 4, capacity, HEAD_DIM), half),
            pltpu.VMEM((chunks, 2, 4, capacity, HEAD_DIM), half),
            pltpu.VMEM((heads, n // GROUPS, 2, tok, HEAD_DIM), half),
            pltpu.VMEM((heads, 4, padded, HEAD_DIM), half),
            pltpu.VMEM((heads, 4, window, HEAD_DIM), half),
            pltpu.VMEM((padded, HEAD_DIM), full),
            pltpu.VMEM((padded, HEAD_DIM), full),
            pltpu.VMEM((tok, LANES), full),
            pltpu.VMEM((tok, LANES), full),
            pltpu.VMEM((n,) + gain_rows, full),
            pltpu.VMEM((n,) + gain_rows, full),
            pltpu.VMEM(gain_rows, full),
            pltpu.VMEM((replicas,) + gain_rows, full),
            pltpu.VMEM(gain_rows, full),
            pltpu.SemaphoreType.DMA((heads,)),
            pltpu.SemaphoreType.DMA((heads,)),
            pltpu.SemaphoreType.DMA((heads,)),
            pltpu.SemaphoreType.DMA((heads,)),
            pltpu.SemaphoreType.DMA((heads,)),
            pltpu.SemaphoreType.DMA((3,)),
            pltpu.SemaphoreType.DMA((3,)),
            pltpu.SemaphoreType.DMA((2, chunks)),
            pltpu.SemaphoreType.DMA((2, chunks)),
            pltpu.SemaphoreType.DMA((2, chunks)),
            pltpu.SemaphoreType.DMA((2, chunks)),
        ],
        compiler_params=pltpu.CompilerParams(
            collective_id=0, has_side_effects=True, vmem_limit_bytes=56 * 1024 * 1024
        ),
    )(
        lengths, q_raw[0], k_raw[0], values[0], grad_out[0],
        q_gain[None], k_gain[None], cosine, sine,
    )
    gains = gains.reshape(n, 2, shared * HEAD_DIM)
    return (
        outs[0][None], outs[1][None], outs[2][None], outs[3][None],
        gains[:, 0].reshape(feature), gains[:, 1].reshape(feature),
    )


def solution(mesh):
    tokens = P("dp", "seq", None)
    return jax.shard_map(
        on_device,
        mesh=mesh,
        in_specs=(tokens, tokens, tokens, tokens, P(), P(), P("dp", None), P("dp", None, "seq")),
        out_specs=(tokens, tokens, tokens, tokens, P(), P()),
        check_vma=False,
    )
```

```python
import functools

import jax
import jax.numpy as jnp
import numpy as np
from jax import lax
from jax.experimental import pallas as pl
from jax.experimental.pallas import tpu as pltpu
from jax.sharding import PartitionSpec as P

HEAD_DIM = 128
LANES = 128
QUERY_BLOCK = 256
GROUPS = 4
CHUNK = 2
TILE = 16
ATTEND_LAG = 2
DISTRIBUTE_LAG = 2
NORM_LAG = 1
DEFERRED = 2
AHEAD = 1
EPSILON = 1e-06
MESH = pl.DeviceIdType.MESH


def rope_constants(head_dim):
    half = head_dim // 2
    sixth = head_dim // 6
    first = half - 2 * sixth
    pairs = np.arange(head_dim) % half
    section = (pairs >= first).astype(np.int32) + (pairs >= first + sixth).astype(np.int32)
    begin = np.where(section == 0, 0, np.where(section == 1, first, first + sixth))
    number = np.where(section == 0, first, sixth)
    freqs = (10000.0 ** (-(pairs - begin) / number)).astype(np.float32)
    return (section == np.arange(3)[:, None]).astype(np.float32) * freqs


def slot_sizes(longest, group_tokens, chunk):
    capacity = TILE
    while True:
        sizes = {n: min(group_tokens, capacity // n // TILE * TILE) for n in range(1, chunk + 1)}

        def fits(below, above):
            return any(
                (n == 0 or below <= sizes[n]) and (n == chunk or above <= sizes[chunk - n])
                for n in range(chunk + 1)
            )

        spill = longest - group_tokens - 1
        if spill <= sizes[chunk] and all(fits(a, longest - a) for a in range(1, longest)):
            return capacity, sizes
        capacity += TILE


def dot(left, right, left_dim, right_dim):
    return lax.dot_general(
        left, right, (((left_dim,), (right_dim,)), ((), ())), preferred_element_type=jnp.float32
    )


def kernel(
    sizes,
    len_ref, q_hbm, k_hbm, v_ref, do_ref, gq_ref, gk_ref, pos_ref, freq_ref,
    att_ref, dq_ref, dk_ref, dv_ref, gain_ref,
    q_ref, k_ref, cos_ref, sin_ref, inner_q, inner_k,
    give, take, give_back, take_back, sent, recv, back, key_acc, value_acc, scale_q, scale_k,
    part, seq_part, dp_sum, dp_part, total,
    raw_sem, in_send, in_recv, own_sem, out_send, out_recv, late_send, late_recv,
    gain_send, gain_recv,
    halo_send, halo_recv, beside_send, beside_recv,
):
    n, replicas, heads, tok, clips, reach, capacity, slots, window, padded = sizes
    members = n // GROUPS
    group_tokens = members * tok
    chunks = heads // CHUNK
    low = [slots[index + 1] for index in range(CHUNK)]
    own_end = [below + group_tokens for below in low]
    feature = members * heads * HEAD_DIM
    ratio = GROUPS
    shared = heads // ratio
    me = lax.axis_index("seq")
    side = me // members
    place_in = lax.rem(me, members)
    my_dp = lax.axis_index("dp")
    scale = HEAD_DIM ** (-0.5)

    def peer(step):
        return lax.rem(me + step, n)

    def member(step):
        return lax.rem(place_in + step, members)

    def device(group, index):
        return (my_dp, group * members + index)

    def columns(owner, head):
        return pl.ds(pl.multiple_of((owner * heads + head) * HEAD_DIM, HEAD_DIM), HEAD_DIM)

    def rows(owner, index):
        return pl.ds(pl.multiple_of(low[index] + owner * tok, TILE), tok)

    def each_side(act):
        @pl.when(side > 0)
        def _():
            act(0, side - 1)

        @pl.when(side < GROUPS - 1)
        def _():
            act(1, side + 1)

    def remote(src, dst, send_sem, recv_sem, device):
        return pltpu.make_async_remote_copy(
            src_ref=src, dst_ref=dst, send_sem=send_sem, recv_sem=recv_sem,
            device_id=device, device_id_type=MESH,
        )

    loads = [
        pltpu.make_async_copy(q_hbm, q_ref, raw_sem.at[0]),
        pltpu.make_async_copy(k_hbm, k_ref, raw_sem.at[1]),
    ]
    for load in loads:
        load.start()

    barrier = pltpu.get_barrier_semaphore()
    for step in range(1, n):
        pl.semaphore_signal(barrier, inc=1, device_id=(my_dp, peer(step)), device_id_type=MESH)
    for step in range(1, replicas):
        other = lax.rem(my_dp + step, replicas)
        pl.semaphore_signal(barrier, inc=1, device_id=(other, me), device_id_type=MESH)
    pl.semaphore_wait(barrier, n - 1 + replicas - 1)

    def send_values(head, index):
        cols = columns(place_in, head)
        for place, ref in ((2, v_ref), (3, do_ref)):
            pltpu.make_async_copy(
                ref.at[:, cols], recv.at[head, place, rows(place_in, index), :], own_sem.at[head]
            ).start()

        @pl.loop(1, members)
        def _(step):
            other = member(step)
            for place, ref in ((2, v_ref), (3, do_ref)):
                remote(
                    ref.at[:, columns(other, head)], recv.at[head, place, rows(place_in, index), :],
                    in_send.at[head], in_recv.at[head], device(side, other),
                ).start()

    ahead = min(AHEAD, chunks)
    for head in range(ahead * CHUNK):
        send_values(head, head % CHUNK)

    held = jnp.concatenate([pos_ref[axis] for axis in range(3)], axis=0)
    angle = lax.dot_general(
        held.astype(jnp.float32), freq_ref[...], (((0,), (0,)), ((), ())),
        precision=lax.Precision.HIGHEST, preferred_element_type=jnp.float32,
    )
    negative = lax.broadcasted_iota(jnp.int32, (tok, HEAD_DIM), 1) < HEAD_DIM // 2
    cos_ref[...] = jnp.cos(angle)
    sine = jnp.sin(angle)
    sin_ref[...] = jnp.where(negative, -sine, sine)
    for load in loads:
        load.wait()

    def squares(index, sums):
        cols = pl.ds(pl.multiple_of(index * LANES, LANES), LANES)
        query = q_ref[:, cols].astype(jnp.float32)
        keys = k_ref[:, cols].astype(jnp.float32)
        return sums[0] + query * query, sums[1] + keys * keys

    zero = jnp.zeros((tok, LANES), jnp.float32)
    sum_q, sum_k = lax.fori_loop(0, feature // LANES, squares, (zero, zero))
    for sums, target in ((sum_q, scale_q), (sum_k, scale_k)):
        mean = jnp.sum(sums, axis=1, keepdims=True) / feature
        target[...] = jnp.broadcast_to(lax.rsqrt(mean + EPSILON), (tok, LANES))

    def rotated(ref, gain, norm, cols):
        x = ref[:, cols].astype(jnp.float32) * norm[...] * gain[:, cols]
        turned = x * cos_ref[...] + pltpu.roll(x, HEAD_DIM // 2, 1) * sin_ref[...]
        return turned.astype(jnp.bfloat16)

    @pl.loop(0, chunks)
    def _(chunk):
        for index in range(CHUNK):
            head = chunk * CHUNK + index

            @pl.loop(1, members)
            def _(step):
                other = member(step)
                cols = columns(other, head)
                sent[head, other, 0] = rotated(q_ref, gq_ref, scale_q, cols)
                sent[head, other, 1] = rotated(k_ref, gk_ref, scale_k, cols)
                remote(
                    sent.at[head, other], recv.at[head, 0:2, rows(place_in, index), :],
                    in_send.at[head], in_recv.at[head], device(side, other),
                ).start()

            cols = columns(place_in, head)
            for place, (ref, gain, norm) in enumerate(
                ((q_ref, gq_ref, scale_q), (k_ref, gk_ref, scale_k))
            ):
                recv[head, place, rows(place_in, index), :] = rotated(ref, gain, norm, cols)

        @pl.when(chunk + ahead < chunks)
        def _():
            for index in range(CHUNK):
                send_values((chunk + ahead) * CHUNK + index, index)

    bounds = []
    running = len_ref[0, 0]
    for clip in range(clips):
        bounds.append(running)
        if clip + 1 < clips:
            running = running + len_ref[0, clip + 1]

    def straddle(middle):
        first, last = jnp.int32(0), jnp.int32(n * tok)
        for bound in bounds:
            first = jnp.maximum(first, jnp.where(bound <= middle, bound, 0))
            last = jnp.minimum(last, jnp.where(bound > middle, bound, n * tok))
        below, above = middle - first, last - middle
        mode = jnp.int32(0)
        for count in range(1, CHUNK + 1):
            fits = below <= slots[count]
            if count < CHUNK:
                fits = fits & (above <= slots[CHUNK - count])
            mode = jnp.where(fits, count, mode)
        return first, last, mode

    token_start = side * group_tokens
    straddles = straddle(token_start), straddle(token_start + group_tokens)

    def clear(index, begin, end):
        @pl.loop(0, chunks)
        def _(chunk):
            recv[chunk * CHUNK + index, :, begin:end, :] = jnp.zeros(
                (4, end - begin, HEAD_DIM), jnp.bfloat16
            )

    for index in range(CHUNK):
        above = own_end[index] + slots[CHUNK - index]
        if padded > above:
            clear(index, above, padded)

        @pl.when(side == 0)
        def _():
            clear(index, 0, low[index])

        @pl.when(side == GROUPS - 1)
        def _():
            clear(index, own_end[index], above)

    def segment(shape, dim, start, shift):
        inside = lax.broadcasted_iota(jnp.int32, shape, dim) + start
        places = inside + (token_start - shift)
        found = jnp.zeros(shape, jnp.int32)
        for bound in bounds:
            found = found + (places >= bound).astype(jnp.int32)
        valid = (inside < window) & (places >= 0) & (places < n * tok)
        return jnp.where(valid, found, -1)

    def taken(upward):
        table = []
        for mode in range(CHUNK + 1):
            if upward:
                size = slots[mode] if mode else 0
                table.append([(index, index * size, size) for index in range(mode)])
            else:
                size = slots[CHUNK - mode] if mode < CHUNK else 0
                table.append([(index, (index - mode) * size, size) for index in range(mode, CHUNK)])
        return table

    def place_of(upward, halo, index, size):
        if upward:
            return (low[index] if halo else own_end[index]) - size
        return own_end[index] if halo else low[index]

    def modes(which):
        held = jnp.full((TILE, HEAD_DIM), straddles[which][2], jnp.int32)
        return [held == mode for mode in range(CHUNK + 1)]

    def gather(target, source, which, upward, halo, chunk):
        masks = modes(which)

        @pl.loop(0, 4)
        def _(place):
            for begin in range(0, capacity, TILE):
                value = None
                for mode, table in enumerate(taken(upward)):
                    for index, start, size in table:
                        if start <= begin < start + size:
                            row = place_of(upward, halo, index, size) + begin - start
                            found = source[chunk * CHUNK + index, place, row:row + TILE, :]
                            value = found if value is None else jnp.where(masks[mode], found, value)
                if value is None:
                    value = jnp.zeros((TILE, HEAD_DIM), jnp.bfloat16)
                target[chunk, which, place, begin:begin + TILE, :] = value

    def scatter(source, target, which, upward, halo, chunk):
        masks = modes(which)
        first, last, mode_now = straddles[which]
        lane_rows = lax.broadcasted_iota(jnp.int32, (TILE, HEAD_DIM), 0)
        limits = []
        for mode in range(CHUNK + 1):
            if upward:
                limits.append(jnp.where(mode_now == mode, first, n * tok))
            else:
                limits.append(jnp.where(mode_now == mode, last, -1))

        @pl.loop(0, 4)
        def _(place):
            for index in range(CHUNK):
                span = slots[index + 1] if upward else slots[CHUNK - index]
                base = place_of(upward, halo, index, span)
                for row in range(base, base + span, TILE):
                    value = None if halo else target[chunk * CHUNK + index, place, row:row + TILE, :]
                    tokens = lane_rows + (token_start + row - low[index])
                    for mode, table in enumerate(taken(upward)):
                        for owner, start, size in table:
                            begin = place_of(upward, halo, owner, size)
                            if owner == index and begin <= row < begin + size:
                                offset = start + row - begin
                                found = source[chunk, which, place, offset:offset + TILE, :]
                                if halo:
                                    mask = masks[mode]
                                elif upward:
                                    mask = tokens >= limits[mode]
                                else:
                                    mask = tokens < limits[mode]
                                value = found if value is None else jnp.where(mask, found, value)
                    target[chunk * CHUNK + index, place, row:row + TILE, :] = value

    def relay(chunk):
        for index in range(CHUNK):
            head = chunk * CHUNK + index
            arrived = recv.at[head, :, pl.ds(0, (members - 1) * tok), :]
            pltpu.make_async_copy(arrived, arrived, in_recv.at[head]).wait()
            own = recv.at[head, pl.ds(2, 2), pl.ds(0, tok), :]
            pltpu.make_async_copy(own, own, own_sem.at[head]).wait()

        def act(which, group):
            gather(give, recv, which, which == 1, False, chunk)
            remote(
                give.at[chunk, which], take.at[chunk, 1 - which],
                halo_send.at[which, chunk], halo_recv.at[1 - which, chunk], device(group, place_in),
            ).start()

        each_side(act)

    def attend(chunk):
        def arrive(which, group):
            held = take.at[chunk, which]
            pltpu.make_async_copy(held, held, halo_recv.at[which, chunk]).wait()
            scatter(take, recv, which, which == 0, True, chunk)

        each_side(arrive)

        @pl.loop(0, CHUNK)
        def _(index):
            shift = jnp.int32(low[0])
            for other in range(1, CHUNK):
                shift = jnp.where(index == other, low[other], shift)
            attend_head(chunk * CHUNK + index, shift)

        def act(which, group):
            gather(give_back, back, which, which == 0, True, chunk)
            remote(
                give_back.at[chunk, which], take_back.at[chunk, 1 - which],
                beside_send.at[which, chunk], beside_recv.at[1 - which, chunk],
                device(group, place_in),
            ).start()

        each_side(act)

    def attend_head(head, shift):
        key_acc[...] = jnp.zeros_like(key_acc)
        value_acc[...] = jnp.zeros_like(value_acc)
        for start in range(0, window, QUERY_BLOCK):
            block = min(QUERY_BLOCK, window - start)
            first = max(0, start - reach) // LANES * LANES
            last = min(padded, -(-(start + block + reach) // LANES) * LANES)
            query = recv[head, 0, start:start + block, :]
            keys = recv[head, 1, first:last, :]
            value_rows = recv[head, 2, first:last, :]
            cot = recv[head, 3, start:start + block, :]
            live = segment((block, 1), 0, start, shift) == segment((1, last - first), 1, first, shift)
            scores = jnp.where(live, dot(query, keys, 1, 1), -1e30)
            highest = jnp.max(scores, axis=1, keepdims=True)
            expon = jnp.exp((scores - highest) * scale)
            probs = expon * (1.0 / jnp.sum(expon, axis=1, keepdims=True))
            half = probs.astype(jnp.bfloat16)
            context = dot(half, value_rows, 1, 0).astype(jnp.bfloat16)
            delta = jnp.sum(
                cot.astype(jnp.float32) * context.astype(jnp.float32), axis=1, keepdims=True
            )
            dprob = dot(cot, value_rows, 1, 1)
            dscore = (probs * (dprob - delta) * scale).astype(jnp.bfloat16)
            back[head, 2, start:start + block, :] = context
            back[head, 0, start:start + block, :] = dot(dscore, keys, 1, 0).astype(jnp.bfloat16)
            key_acc[first:last, :] += dot(dscore, query, 0, 0)
            value_acc[first:last, :] += dot(half, cot, 0, 0)
        back[head, 1] = key_acc[0:window, :].astype(jnp.bfloat16)
        back[head, 3] = value_acc[0:window, :].astype(jnp.bfloat16)

    def distribute(chunk):
        def merge(which, group):
            held = take_back.at[chunk, which]
            pltpu.make_async_copy(held, held, beside_recv.at[which, chunk]).wait()
            scatter(take_back, back, which, which == 1, False, chunk)

        each_side(merge)
        outward(chunk, 0, (dq_ref, dk_ref), out_send, out_recv)

        @pl.when(chunk < chunks - DEFERRED)
        def _():
            outward(chunk, 2, (att_ref, dv_ref), late_send, late_recv)

    def outward(chunk, first, targets, send, receive):
        for index in range(CHUNK):
            head = chunk * CHUNK + index
            cols = columns(place_in, head)

            @pl.loop(1, members)
            def _(step):
                other = member(step)
                for place, target in enumerate(targets):
                    remote(
                        back.at[head, first + place, rows(other, index), :], target.at[:, cols],
                        send.at[head], receive.at[head], device(side, other),
                    ).start()

            for place, target in enumerate(targets):
                target[:, cols] = back[head, first + place, rows(place_in, index), :]

    def arrived_pair(head, sem):
        held = recv.at[head, 0:2, pl.ds(0, (members - 1) * tok), :]
        pltpu.make_async_copy(held, held, sem.at[head]).wait()

    def turned_back(grad, ref, norm, cols):
        grads = grad[:, cols].astype(jnp.float32)
        turned = grads * cos_ref[...] - pltpu.roll(grads, HEAD_DIM // 2, 1) * sin_ref[...]
        return turned, ref[:, cols].astype(jnp.float32) * norm[...]

    sides = (
        (dq_ref, q_ref, gq_ref, scale_q, inner_q), (dk_ref, k_ref, gk_ref, scale_k, inner_k),
    )
    inner_q[...] = zero
    inner_k[...] = zero

    def first_pass(chunk):
        for index in range(CHUNK):
            head = chunk * CHUNK + index
            arrived_pair(head, out_recv)

            @pl.loop(0, members)
            def _(owner):
                cols = columns(owner, head)
                for place, (grad, ref, gain, norm, inner) in enumerate(sides):
                    turned, hat = turned_back(grad, ref, norm, cols)
                    both = turned * hat
                    row = place * shared + lax.rem(head, shared)
                    part[owner * ratio + head // shared, pl.ds(row, 1), :] = jnp.sum(
                        both, axis=0, keepdims=True
                    )
                    inner[...] += both * gain[:, cols]

    @pl.loop(0, chunks + ATTEND_LAG + DISTRIBUTE_LAG + NORM_LAG)
    def _(step):
        @pl.when(step < chunks)
        def _():
            relay(step)

        @pl.when((step >= ATTEND_LAG) & (step < chunks + ATTEND_LAG))
        def _():
            attend(step - ATTEND_LAG)

        @pl.when(
            (step >= ATTEND_LAG + DISTRIBUTE_LAG) & (step < chunks + ATTEND_LAG + DISTRIBUTE_LAG)
        )
        def _():
            distribute(step - ATTEND_LAG - DISTRIBUTE_LAG)

        @pl.when(step >= ATTEND_LAG + DISTRIBUTE_LAG + NORM_LAG)
        def _():
            first_pass(step - ATTEND_LAG - DISTRIBUTE_LAG - NORM_LAG)

    per = n // replicas

    def portion(index):
        return pl.ds(index * per, per)

    for step in range(1, replicas):
        other = lax.rem(my_dp + step, replicas)
        remote(
            part.at[portion(other)], dp_part.at[my_dp], gain_send.at[0], gain_recv.at[0], (other, me)
        ).start()
    dp_part[my_dp] = part[portion(my_dp)]

    @pl.loop(chunks - min(DEFERRED, chunks), chunks)
    def _(chunk):
        outward(chunk, 2, (att_ref, dv_ref), late_send, late_recv)

    means = [
        jnp.broadcast_to(jnp.sum(inner[...], axis=1, keepdims=True) / feature, (tok, LANES))
        for inner in (inner_q, inner_k)
    ]

    def second_pass(index):
        cols = pl.ds(pl.multiple_of(index * LANES, LANES), LANES)
        for (grad, ref, gain, norm, _), mean in zip(sides, means):
            turned, hat = turned_back(grad, ref, norm, cols)
            result = norm[...] * (turned * gain[:, cols] - hat * mean)
            grad[:, cols] = result.astype(jnp.bfloat16)

    pl.loop(0, feature // LANES)(second_pass)

    def wait_all(ref, count, sem):
        held = ref.at[pl.ds(0, count)]
        pltpu.make_async_copy(held, held, sem).wait()

    wait_all(dp_part, replicas - 1, gain_recv.at[0])
    dp_sum[...] = jnp.sum(dp_part[...], axis=0)

    @pl.loop(1, n)
    def _(step):
        other = peer(step)
        remote(
            dp_sum, seq_part.at[me], gain_send.at[1], gain_recv.at[1], (my_dp, other)
        ).start()

    seq_part[me] = dp_sum[...]
    wait_all(seq_part, n - 1, gain_recv.at[1])
    total[...] = jnp.sum(seq_part[...], axis=0) / replicas
    for step in range(1, replicas):
        other = lax.rem(my_dp + step, replicas)
        remote(
            total, gain_ref.at[portion(my_dp)], gain_send.at[2], gain_recv.at[2], (other, me)
        ).start()
    gain_ref[portion(my_dp)] = total[...]
    wait_all(dp_part, replicas - 1, gain_recv.at[2])

    wait_all(dp_part, replicas - 1, gain_send.at[0])
    wait_all(seq_part, n - 1, gain_send.at[1])
    wait_all(dp_part, replicas - 1, gain_send.at[2])

    @pl.loop(0, heads)
    def _(head):
        moved = recv.at[head, :, pl.ds(0, (members - 1) * tok), :]
        pltpu.make_async_copy(moved, moved, in_send.at[head]).wait()
        arrived_pair(head, out_send)
        arrived_pair(head, late_send)
        arrived_pair(head, late_recv)

    @pl.loop(0, chunks)
    def _(chunk):
        def drain(which, group):
            held = give.at[chunk, which]
            pltpu.make_async_copy(held, held, halo_send.at[which, chunk]).wait()
            pltpu.make_async_copy(held, held, beside_send.at[which, chunk]).wait()

        each_side(drain)


def finish(gains_ref, *refs):
    arrays, targets, (gq_ref, gk_ref), sems = refs[:4], refs[4:8], refs[8:10], refs[10]
    copies = [
        pltpu.make_async_copy(source, target, sems.at[index])
        for index, (source, target) in enumerate(zip(arrays, targets))
    ]
    for copy in copies:
        copy.start()
    owners, shared = gains_ref.shape[0], gains_ref.shape[1] // 2
    for owner in range(owners):
        for row in range(shared):
            cols = slice((owner * shared + row) * LANES, (owner * shared + row + 1) * LANES)
            gq_ref[:, cols] = gains_ref[owner, row:row + 1, :]
            gk_ref[:, cols] = gains_ref[owner, shared + row:shared + row + 1, :]
    for copy in copies:
        copy.wait()


def on_device(q_raw, k_raw, values, grad_out, q_gain, k_gain, lengths, positions):
    n = lax.axis_size("seq")
    replicas = lax.axis_size("dp")
    tok, feature = q_raw.shape[1:]
    shared = feature // n // HEAD_DIM
    heads = GROUPS * shared
    tokens = n * tok
    reach = tokens // 3 - 1
    group_tokens = tokens // GROUPS
    chunks = heads // CHUNK
    capacity, slots = slot_sizes(reach + 1, group_tokens, CHUNK)
    window = group_tokens + max(slots[i + 1] + slots[CHUNK - i] for i in range(CHUNK))
    padded = -(-window // LANES) * LANES
    sizes = (n, replicas, heads, tok, lengths.shape[1], reach, capacity, slots, window, padded)
    vmem = pl.BlockSpec(memory_space=pltpu.VMEM)
    hbm = pl.BlockSpec(memory_space=pl.ANY)
    gain_rows = (2 * shared, LANES)
    half, full = jnp.bfloat16, jnp.float32
    *outs, gains = pl.pallas_call(
        functools.partial(kernel, sizes),
        out_shape=(
            *[pltpu.VMEM((tok, feature), half)] * 4,
            pltpu.VMEM((n,) + gain_rows, full),
        ),
        in_specs=[
            pl.BlockSpec(memory_space=pltpu.SMEM), hbm, hbm, hbm, hbm, vmem, vmem, vmem, vmem,
        ],
        out_specs=(vmem,) * 5,
        scratch_shapes=[
            pltpu.VMEM((tok, feature), half),
            pltpu.VMEM((tok, feature), half),
            pltpu.VMEM((tok, HEAD_DIM), full),
            pltpu.VMEM((tok, HEAD_DIM), full),
            pltpu.VMEM((tok, LANES), full),
            pltpu.VMEM((tok, LANES), full),
            pltpu.VMEM((chunks, 2, 4, capacity, HEAD_DIM), half),
            pltpu.VMEM((chunks, 2, 4, capacity, HEAD_DIM), half),
            pltpu.VMEM((chunks, 2, 4, capacity, HEAD_DIM), half),
            pltpu.VMEM((chunks, 2, 4, capacity, HEAD_DIM), half),
            pltpu.VMEM((heads, n // GROUPS, 2, tok, HEAD_DIM), half),
            pltpu.VMEM((heads, 4, padded, HEAD_DIM), half),
            pltpu.VMEM((heads, 4, window, HEAD_DIM), half),
            pltpu.VMEM((padded, HEAD_DIM), full),
            pltpu.VMEM((padded, HEAD_DIM), full),
            pltpu.VMEM((tok, LANES), full),
            pltpu.VMEM((tok, LANES), full),
            pltpu.VMEM((n,) + gain_rows, full),
            pltpu.VMEM((n, n // replicas) + gain_rows, full),
            pltpu.VMEM((n // replicas,) + gain_rows, full),
            pltpu.VMEM((replicas, n // replicas) + gain_rows, full),
            pltpu.VMEM((n // replicas,) + gain_rows, full),
            pltpu.SemaphoreType.DMA((2,)),
            pltpu.SemaphoreType.DMA((heads,)),
            pltpu.SemaphoreType.DMA((heads,)),
            pltpu.SemaphoreType.DMA((heads,)),
            pltpu.SemaphoreType.DMA((heads,)),
            pltpu.SemaphoreType.DMA((heads,)),
            pltpu.SemaphoreType.DMA((heads,)),
            pltpu.SemaphoreType.DMA((heads,)),
            pltpu.SemaphoreType.DMA((3,)),
            pltpu.SemaphoreType.DMA((3,)),
            pltpu.SemaphoreType.DMA((2, chunks)),
            pltpu.SemaphoreType.DMA((2, chunks)),
            pltpu.SemaphoreType.DMA((2, chunks)),
            pltpu.SemaphoreType.DMA((2, chunks)),
        ],
        compiler_params=pltpu.CompilerParams(
            collective_id=0, has_side_effects=True, vmem_limit_bytes=56 * 1024 * 1024
        ),
    )(
        lengths, q_raw[0], k_raw[0], values[0], grad_out[0],
        q_gain[None], k_gain[None], positions[0][:, None], jnp.asarray(rope_constants(HEAD_DIM)),
    )
    attended, grad_q, grad_k, grad_v, gain_q, gain_k = pl.pallas_call(
        finish,
        out_shape=(jax.ShapeDtypeStruct((tok, feature), half),) * 4
        + (jax.ShapeDtypeStruct((1, feature), full),) * 2,
        in_specs=[vmem] * 5,
        out_specs=(hbm,) * 4 + (vmem,) * 2,
        scratch_shapes=[pltpu.SemaphoreType.DMA((4,))],
        compiler_params=pltpu.CompilerParams(vmem_limit_bytes=6 * 1024 * 1024),
    )(gains, *outs)
    return (
        attended[None], grad_q[None], grad_k[None], grad_v[None], gain_q[0], gain_k[0],
    )


def solution(mesh):
    tokens = P("dp", "seq", None)
    return jax.shard_map(
        on_device,
        mesh=mesh,
        in_specs=(tokens, tokens, tokens, tokens, P(), P(), P("dp", None), P("dp", None, "seq")),
        out_specs=(tokens, tokens, tokens, tokens, P(), P()),
        check_vma=False,
    )
```

```python
import functools

import jax
import jax.numpy as jnp
import numpy as np
from jax import lax
from jax.experimental import pallas as pl
from jax.experimental.pallas import tpu as pltpu
from jax.sharding import PartitionSpec as P

HEAD_DIM = 128
LANES = 128
QUERY_BLOCK = 256
GROUPS = 4
CHUNK = 2
TILE = 16
ATTEND_LAG = 2
DISTRIBUTE_LAG = 2
NORM_LAG = 1
DEFERRED = 2
AHEAD = 1
EPSILON = 1e-06
MESH = pl.DeviceIdType.MESH


def rope_constants(head_dim):
    half = head_dim // 2
    sixth = head_dim // 6
    first = half - 2 * sixth
    pairs = np.arange(head_dim) % half
    section = (pairs >= first).astype(np.int32) + (pairs >= first + sixth).astype(np.int32)
    begin = np.where(section == 0, 0, np.where(section == 1, first, first + sixth))
    number = np.where(section == 0, first, sixth)
    freqs = (10000.0 ** (-(pairs - begin) / number)).astype(np.float32)
    return (section == np.arange(3)[:, None]).astype(np.float32) * freqs


def slot_sizes(longest, group_tokens, chunk):
    capacity = TILE
    while True:
        sizes = {n: min(group_tokens, capacity // n // TILE * TILE) for n in range(1, chunk + 1)}

        def fits(below, above):
            return any(
                (n == 0 or below <= sizes[n]) and (n == chunk or above <= sizes[chunk - n])
                for n in range(chunk + 1)
            )

        spill = longest - group_tokens - 1
        if spill <= sizes[chunk] and all(fits(a, longest - a) for a in range(1, longest)):
            return capacity, sizes
        capacity += TILE


def dot(left, right, left_dim, right_dim):
    return lax.dot_general(
        left, right, (((left_dim,), (right_dim,)), ((), ())), preferred_element_type=jnp.float32
    )


def kernel(
    sizes,
    len_ref, q_hbm, k_hbm, v_ref, do_ref, gq_ref, gk_ref, pos_ref, freq_ref,
    att_ref, dq_ref, dk_ref, dv_ref, gain_ref,
    q_ref, k_ref, cos_ref, sin_ref, inner_q, inner_k,
    give, take, give_back, take_back, sent, recv, back, key_acc, value_acc, scale_q, scale_k,
    part, seq_part, dp_sum, dp_part, total,
    raw_sem, in_send, in_recv, own_sem, out_send, out_recv, late_send, late_recv,
    gain_send, gain_recv,
    halo_send, halo_recv, beside_send, beside_recv,
):
    n, replicas, heads, tok, clips, reach, capacity, slots, window, padded = sizes
    members = n // GROUPS
    group_tokens = members * tok
    chunks = heads // CHUNK
    low = [slots[index + 1] for index in range(CHUNK)]
    own_end = [below + group_tokens for below in low]
    feature = members * heads * HEAD_DIM
    ratio = GROUPS
    shared = heads // ratio
    me = lax.axis_index("seq")
    side = me // members
    place_in = lax.rem(me, members)
    my_dp = lax.axis_index("dp")
    scale = HEAD_DIM ** (-0.5)

    def peer(step):
        return lax.rem(me + step, n)

    def member(step):
        return lax.rem(place_in + step, members)

    def device(group, index):
        return (my_dp, group * members + index)

    def columns(owner, head):
        return pl.ds(pl.multiple_of((owner * heads + head) * HEAD_DIM, HEAD_DIM), HEAD_DIM)

    def rows(owner, index):
        return pl.ds(pl.multiple_of(low[index] + owner * tok, TILE), tok)

    def each_side(act):
        @pl.when(side > 0)
        def _():
            act(0, side - 1)

        @pl.when(side < GROUPS - 1)
        def _():
            act(1, side + 1)

    def remote(src, dst, send_sem, recv_sem, device):
        return pltpu.make_async_remote_copy(
            src_ref=src, dst_ref=dst, send_sem=send_sem, recv_sem=recv_sem,
            device_id=device, device_id_type=MESH,
        )

    loads = [
        pltpu.make_async_copy(q_hbm, q_ref, raw_sem.at[0]),
        pltpu.make_async_copy(k_hbm, k_ref, raw_sem.at[1]),
    ]
    for load in loads:
        load.start()

    barrier = pltpu.get_barrier_semaphore()

    def greet(target):
        pl.semaphore_signal(barrier, inc=1, device_id=target, device_id_type=MESH)

    for step in range(1, members):
        greet(device(side, member(step)))
    for step in range(1, replicas):
        greet((lax.rem(my_dp + step, replicas), me))
    each_side(lambda which, group: greet(device(group, place_in)))
    sides_here = jnp.minimum(side, 1) + jnp.minimum(GROUPS - 1 - side, 1)
    pl.semaphore_wait(barrier, members - 1 + replicas - 1 + sides_here)

    def send_values(head, index):
        cols = columns(place_in, head)
        for place, ref in ((2, v_ref), (3, do_ref)):
            pltpu.make_async_copy(
                ref.at[:, cols], recv.at[head, place, rows(place_in, index), :], own_sem.at[head]
            ).start()

        @pl.loop(1, members)
        def _(step):
            other = member(step)
            for place, ref in ((2, v_ref), (3, do_ref)):
                remote(
                    ref.at[:, columns(other, head)], recv.at[head, place, rows(place_in, index), :],
                    in_send.at[head], in_recv.at[head], device(side, other),
                ).start()

    ahead = min(AHEAD, chunks)
    for head in range(ahead * CHUNK):
        send_values(head, head % CHUNK)

    held = jnp.concatenate([pos_ref[axis] for axis in range(3)], axis=0)
    angle = lax.dot_general(
        held.astype(jnp.float32), freq_ref[...], (((0,), (0,)), ((), ())),
        precision=lax.Precision.HIGHEST, preferred_element_type=jnp.float32,
    )
    negative = lax.broadcasted_iota(jnp.int32, (tok, HEAD_DIM), 1) < HEAD_DIM // 2
    cos_ref[...] = jnp.cos(angle)
    sine = jnp.sin(angle)
    sin_ref[...] = jnp.where(negative, -sine, sine)
    for load in loads:
        load.wait()

    def squares(index, sums):
        cols = pl.ds(pl.multiple_of(index * LANES, LANES), LANES)
        query = q_ref[:, cols].astype(jnp.float32)
        keys = k_ref[:, cols].astype(jnp.float32)
        return sums[0] + query * query, sums[1] + keys * keys

    zero = jnp.zeros((tok, LANES), jnp.float32)
    sum_q, sum_k = lax.fori_loop(0, feature // LANES, squares, (zero, zero))
    for sums, target in ((sum_q, scale_q), (sum_k, scale_k)):
        mean = jnp.sum(sums, axis=1, keepdims=True) / feature
        target[...] = jnp.broadcast_to(lax.rsqrt(mean + EPSILON), (tok, LANES))

    def rotated(ref, gain, norm, cols):
        x = ref[:, cols].astype(jnp.float32) * norm[...] * gain[:, cols]
        turned = x * cos_ref[...] + pltpu.roll(x, HEAD_DIM // 2, 1) * sin_ref[...]
        return turned.astype(jnp.bfloat16)

    @pl.loop(0, chunks)
    def _(chunk):
        for index in range(CHUNK):
            head = chunk * CHUNK + index

            @pl.loop(1, members)
            def _(step):
                other = member(step)
                cols = columns(other, head)
                sent[head, other, 0] = rotated(q_ref, gq_ref, scale_q, cols)
                sent[head, other, 1] = rotated(k_ref, gk_ref, scale_k, cols)
                remote(
                    sent.at[head, other], recv.at[head, 0:2, rows(place_in, index), :],
                    in_send.at[head], in_recv.at[head], device(side, other),
                ).start()

            cols = columns(place_in, head)
            for place, (ref, gain, norm) in enumerate(
                ((q_ref, gq_ref, scale_q), (k_ref, gk_ref, scale_k))
            ):
                recv[head, place, rows(place_in, index), :] = rotated(ref, gain, norm, cols)

        @pl.when(chunk + ahead < chunks)
        def _():
            for index in range(CHUNK):
                send_values((chunk + ahead) * CHUNK + index, index)

    bounds = []
    running = len_ref[0, 0]
    for clip in range(clips):
        bounds.append(running)
        if clip + 1 < clips:
            running = running + len_ref[0, clip + 1]

    def straddle(middle):
        first, last = jnp.int32(0), jnp.int32(n * tok)
        for bound in bounds:
            first = jnp.maximum(first, jnp.where(bound <= middle, bound, 0))
            last = jnp.minimum(last, jnp.where(bound > middle, bound, n * tok))
        below, above = middle - first, last - middle
        mode = jnp.int32(0)
        for count in range(1, CHUNK + 1):
            fits = below <= slots[count]
            if count < CHUNK:
                fits = fits & (above <= slots[CHUNK - count])
            mode = jnp.where(fits, count, mode)
        return first, last, mode

    token_start = side * group_tokens
    straddles = straddle(token_start), straddle(token_start + group_tokens)

    def clear(index, begin, end):
        @pl.loop(0, chunks)
        def _(chunk):
            recv[chunk * CHUNK + index, :, begin:end, :] = jnp.zeros(
                (4, end - begin, HEAD_DIM), jnp.bfloat16
            )

    for index in range(CHUNK):
        above = own_end[index] + slots[CHUNK - index]
        if padded > above:
            clear(index, above, padded)

        @pl.when(side == 0)
        def _():
            clear(index, 0, low[index])

        @pl.when(side == GROUPS - 1)
        def _():
            clear(index, own_end[index], above)

    def segment(shape, dim, start, shift):
        inside = lax.broadcasted_iota(jnp.int32, shape, dim) + start
        places = inside + (token_start - shift)
        found = jnp.zeros(shape, jnp.int32)
        for bound in bounds:
            found = found + (places >= bound).astype(jnp.int32)
        valid = (inside < window) & (places >= 0) & (places < n * tok)
        return jnp.where(valid, found, -1)

    def taken(upward):
        table = []
        for mode in range(CHUNK + 1):
            if upward:
                size = slots[mode] if mode else 0
                table.append([(index, index * size, size) for index in range(mode)])
            else:
                size = slots[CHUNK - mode] if mode < CHUNK else 0
                table.append([(index, (index - mode) * size, size) for index in range(mode, CHUNK)])
        return table

    def place_of(upward, halo, index, size):
        if upward:
            return (low[index] if halo else own_end[index]) - size
        return own_end[index] if halo else low[index]

    def modes(which):
        held = jnp.full((TILE, HEAD_DIM), straddles[which][2], jnp.int32)
        return [held == mode for mode in range(CHUNK + 1)]

    def gather(target, source, which, upward, halo, chunk):
        masks = modes(which)

        @pl.loop(0, 4)
        def _(place):
            for begin in range(0, capacity, TILE):
                value = None
                for mode, table in enumerate(taken(upward)):
                    for index, start, size in table:
                        if start <= begin < start + size:
                            row = place_of(upward, halo, index, size) + begin - start
                            found = source[chunk * CHUNK + index, place, row:row + TILE, :]
                            value = found if value is None else jnp.where(masks[mode], found, value)
                if value is None:
                    value = jnp.zeros((TILE, HEAD_DIM), jnp.bfloat16)
                target[chunk, which, place, begin:begin + TILE, :] = value

    def scatter(source, target, which, upward, halo, chunk):
        masks = modes(which)
        first, last, mode_now = straddles[which]
        lane_rows = lax.broadcasted_iota(jnp.int32, (TILE, HEAD_DIM), 0)
        limits = []
        for mode in range(CHUNK + 1):
            if upward:
                limits.append(jnp.where(mode_now == mode, first, n * tok))
            else:
                limits.append(jnp.where(mode_now == mode, last, -1))

        @pl.loop(0, 4)
        def _(place):
            for index in range(CHUNK):
                span = slots[index + 1] if upward else slots[CHUNK - index]
                base = place_of(upward, halo, index, span)
                for row in range(base, base + span, TILE):
                    value = None if halo else target[chunk * CHUNK + index, place, row:row + TILE, :]
                    tokens = lane_rows + (token_start + row - low[index])
                    for mode, table in enumerate(taken(upward)):
                        for owner, start, size in table:
                            begin = place_of(upward, halo, owner, size)
                            if owner == index and begin <= row < begin + size:
                                offset = start + row - begin
                                found = source[chunk, which, place, offset:offset + TILE, :]
                                if halo:
                                    mask = masks[mode]
                                elif upward:
                                    mask = tokens >= limits[mode]
                                else:
                                    mask = tokens < limits[mode]
                                value = found if value is None else jnp.where(mask, found, value)
                    target[chunk * CHUNK + index, place, row:row + TILE, :] = value

    def relay(chunk):
        for index in range(CHUNK):
            head = chunk * CHUNK + index
            arrived = recv.at[head, :, pl.ds(0, (members - 1) * tok), :]
            pltpu.make_async_copy(arrived, arrived, in_recv.at[head]).wait()
            own = recv.at[head, pl.ds(2, 2), pl.ds(0, tok), :]
            pltpu.make_async_copy(own, own, own_sem.at[head]).wait()

        def act(which, group):
            gather(give, recv, which, which == 1, False, chunk)
            remote(
                give.at[chunk, which], take.at[chunk, 1 - which],
                halo_send.at[which, chunk], halo_recv.at[1 - which, chunk], device(group, place_in),
            ).start()

        each_side(act)

    def attend(chunk):
        def arrive(which, group):
            held = take.at[chunk, which]
            pltpu.make_async_copy(held, held, halo_recv.at[which, chunk]).wait()
            scatter(take, recv, which, which == 0, True, chunk)

        each_side(arrive)

        @pl.loop(0, CHUNK)
        def _(index):
            shift = jnp.int32(low[0])
            for other in range(1, CHUNK):
                shift = jnp.where(index == other, low[other], shift)
            attend_head(chunk * CHUNK + index, shift)

        def act(which, group):
            gather(give_back, back, which, which == 0, True, chunk)
            remote(
                give_back.at[chunk, which], take_back.at[chunk, 1 - which],
                beside_send.at[which, chunk], beside_recv.at[1 - which, chunk],
                device(group, place_in),
            ).start()

        each_side(act)

    def attend_head(head, shift):
        key_acc[...] = jnp.zeros_like(key_acc)
        value_acc[...] = jnp.zeros_like(value_acc)
        for start in range(0, window, QUERY_BLOCK):
            block = min(QUERY_BLOCK, window - start)
            first = max(0, start - reach) // LANES * LANES
            last = min(padded, -(-(start + block + reach) // LANES) * LANES)
            query = recv[head, 0, start:start + block, :]
            keys = recv[head, 1, first:last, :]
            value_rows = recv[head, 2, first:last, :]
            cot = recv[head, 3, start:start + block, :]
            live = segment((block, 1), 0, start, shift) == segment((1, last - first), 1, first, shift)
            scores = jnp.where(live, dot(query, keys, 1, 1), -1e30)
            highest = jnp.max(scores, axis=1, keepdims=True)
            expon = jnp.exp((scores - highest) * scale)
            probs = expon * (1.0 / jnp.sum(expon, axis=1, keepdims=True))
            half = probs.astype(jnp.bfloat16)
            context = dot(half, value_rows, 1, 0).astype(jnp.bfloat16)
            delta = jnp.sum(
                cot.astype(jnp.float32) * context.astype(jnp.float32), axis=1, keepdims=True
            )
            dprob = dot(cot, value_rows, 1, 1)
            dscore = (probs * (dprob - delta) * scale).astype(jnp.bfloat16)
            back[head, 2, start:start + block, :] = context
            back[head, 0, start:start + block, :] = dot(dscore, keys, 1, 0).astype(jnp.bfloat16)
            key_acc[first:last, :] += dot(dscore, query, 0, 0)
            value_acc[first:last, :] += dot(half, cot, 0, 0)
        back[head, 1] = key_acc[0:window, :].astype(jnp.bfloat16)
        back[head, 3] = value_acc[0:window, :].astype(jnp.bfloat16)

    def distribute(chunk):
        def merge(which, group):
            held = take_back.at[chunk, which]
            pltpu.make_async_copy(held, held, beside_recv.at[which, chunk]).wait()
            scatter(take_back, back, which, which == 1, False, chunk)

        each_side(merge)
        outward(chunk, 0, (dq_ref, dk_ref), out_send, out_recv)

        @pl.when(chunk < chunks - DEFERRED)
        def _():
            outward(chunk, 2, (att_ref, dv_ref), late_send, late_recv)

    def outward(chunk, first, targets, send, receive):
        for index in range(CHUNK):
            head = chunk * CHUNK + index
            cols = columns(place_in, head)

            @pl.loop(1, members)
            def _(step):
                other = member(step)
                for place, target in enumerate(targets):
                    remote(
                        back.at[head, first + place, rows(other, index), :], target.at[:, cols],
                        send.at[head], receive.at[head], device(side, other),
                    ).start()

            for place, target in enumerate(targets):
                target[:, cols] = back[head, first + place, rows(place_in, index), :]

    def arrived_pair(head, sem):
        held = recv.at[head, 0:2, pl.ds(0, (members - 1) * tok), :]
        pltpu.make_async_copy(held, held, sem.at[head]).wait()

    def turned_back(grad, ref, norm, cols):
        grads = grad[:, cols].astype(jnp.float32)
        turned = grads * cos_ref[...] - pltpu.roll(grads, HEAD_DIM // 2, 1) * sin_ref[...]
        return turned, ref[:, cols].astype(jnp.float32) * norm[...]

    sides = (
        (dq_ref, q_ref, gq_ref, scale_q, inner_q), (dk_ref, k_ref, gk_ref, scale_k, inner_k),
    )
    inner_q[...] = zero
    inner_k[...] = zero

    def first_pass(chunk):
        for index in range(CHUNK):
            head = chunk * CHUNK + index
            arrived_pair(head, out_recv)

            @pl.loop(0, members)
            def _(owner):
                cols = columns(owner, head)
                for place, (grad, ref, gain, norm, inner) in enumerate(sides):
                    turned, hat = turned_back(grad, ref, norm, cols)
                    both = turned * hat
                    row = place * shared + lax.rem(head, shared)
                    part[owner * ratio + head // shared, pl.ds(row, 1), :] = jnp.sum(
                        both, axis=0, keepdims=True
                    )
                    inner[...] += both * gain[:, cols]

    @pl.loop(0, chunks + ATTEND_LAG + DISTRIBUTE_LAG + NORM_LAG)
    def _(step):
        @pl.when(step < chunks)
        def _():
            relay(step)

        @pl.when((step >= ATTEND_LAG) & (step < chunks + ATTEND_LAG))
        def _():
            attend(step - ATTEND_LAG)

        @pl.when(
            (step >= ATTEND_LAG + DISTRIBUTE_LAG) & (step < chunks + ATTEND_LAG + DISTRIBUTE_LAG)
        )
        def _():
            distribute(step - ATTEND_LAG - DISTRIBUTE_LAG)

        @pl.when(step >= ATTEND_LAG + DISTRIBUTE_LAG + NORM_LAG)
        def _():
            first_pass(step - ATTEND_LAG - DISTRIBUTE_LAG - NORM_LAG)

    per = n // replicas

    def portion(index):
        return pl.ds(index * per, per)

    for step in range(1, replicas):
        other = lax.rem(my_dp + step, replicas)
        remote(
            part.at[portion(other)], dp_part.at[my_dp], gain_send.at[0], gain_recv.at[0], (other, me)
        ).start()
    dp_part[my_dp] = part[portion(my_dp)]

    @pl.loop(chunks - min(DEFERRED, chunks), chunks)
    def _(chunk):
        outward(chunk, 2, (att_ref, dv_ref), late_send, late_recv)

    means = [
        jnp.broadcast_to(jnp.sum(inner[...], axis=1, keepdims=True) / feature, (tok, LANES))
        for inner in (inner_q, inner_k)
    ]

    def second_pass(index):
        cols = pl.ds(pl.multiple_of(index * LANES, LANES), LANES)
        for (grad, ref, gain, norm, _), mean in zip(sides, means):
            turned, hat = turned_back(grad, ref, norm, cols)
            result = norm[...] * (turned * gain[:, cols] - hat * mean)
            grad[:, cols] = result.astype(jnp.bfloat16)

    pl.loop(0, feature // LANES)(second_pass)

    def wait_all(ref, count, sem):
        held = ref.at[pl.ds(0, count)]
        pltpu.make_async_copy(held, held, sem).wait()

    wait_all(dp_part, replicas - 1, gain_recv.at[0])
    dp_sum[...] = jnp.sum(dp_part[...], axis=0)

    @pl.loop(1, n)
    def _(step):
        other = peer(step)
        remote(
            dp_sum, seq_part.at[me], gain_send.at[1], gain_recv.at[1], (my_dp, other)
        ).start()

    seq_part[me] = dp_sum[...]
    wait_all(seq_part, n - 1, gain_recv.at[1])
    total[...] = jnp.sum(seq_part[...], axis=0) / replicas
    for step in range(1, replicas):
        other = lax.rem(my_dp + step, replicas)
        remote(
            total, gain_ref.at[portion(my_dp)], gain_send.at[2], gain_recv.at[2], (other, me)
        ).start()
    gain_ref[portion(my_dp)] = total[...]
    wait_all(dp_part, replicas - 1, gain_recv.at[2])

    wait_all(dp_part, replicas - 1, gain_send.at[0])
    wait_all(seq_part, n - 1, gain_send.at[1])
    wait_all(dp_part, replicas - 1, gain_send.at[2])

    @pl.loop(0, heads)
    def _(head):
        moved = recv.at[head, :, pl.ds(0, (members - 1) * tok), :]
        pltpu.make_async_copy(moved, moved, in_send.at[head]).wait()
        arrived_pair(head, out_send)
        arrived_pair(head, late_send)
        arrived_pair(head, late_recv)

    @pl.loop(0, chunks)
    def _(chunk):
        def drain(which, group):
            held = give.at[chunk, which]
            pltpu.make_async_copy(held, held, halo_send.at[which, chunk]).wait()
            pltpu.make_async_copy(held, held, beside_send.at[which, chunk]).wait()

        each_side(drain)


def finish(gains_ref, *refs):
    arrays, targets, (gq_ref, gk_ref), sems = refs[:4], refs[4:8], refs[8:10], refs[10]
    copies = [
        pltpu.make_async_copy(source, target, sems.at[index])
        for index, (source, target) in enumerate(zip(arrays, targets))
    ]
    for copy in copies:
        copy.start()
    owners, shared = gains_ref.shape[0], gains_ref.shape[1] // 2
    for owner in range(owners):
        for row in range(shared):
            cols = slice((owner * shared + row) * LANES, (owner * shared + row + 1) * LANES)
            gq_ref[:, cols] = gains_ref[owner, row:row + 1, :]
            gk_ref[:, cols] = gains_ref[owner, shared + row:shared + row + 1, :]
    for copy in copies:
        copy.wait()


def on_device(q_raw, k_raw, values, grad_out, q_gain, k_gain, lengths, positions):
    n = lax.axis_size("seq")
    replicas = lax.axis_size("dp")
    tok, feature = q_raw.shape[1:]
    shared = feature // n // HEAD_DIM
    heads = GROUPS * shared
    tokens = n * tok
    reach = tokens // 3 - 1
    group_tokens = tokens // GROUPS
    chunks = heads // CHUNK
    capacity, slots = slot_sizes(reach + 1, group_tokens, CHUNK)
    window = group_tokens + max(slots[i + 1] + slots[CHUNK - i] for i in range(CHUNK))
    padded = -(-window // LANES) * LANES
    sizes = (n, replicas, heads, tok, lengths.shape[1], reach, capacity, slots, window, padded)
    vmem = pl.BlockSpec(memory_space=pltpu.VMEM)
    hbm = pl.BlockSpec(memory_space=pl.ANY)
    gain_rows = (2 * shared, LANES)
    half, full = jnp.bfloat16, jnp.float32
    *outs, gains = pl.pallas_call(
        functools.partial(kernel, sizes),
        out_shape=(
            *[pltpu.VMEM((tok, feature), half)] * 4,
            pltpu.VMEM((n,) + gain_rows, full),
        ),
        in_specs=[
            pl.BlockSpec(memory_space=pltpu.SMEM), hbm, hbm, hbm, hbm, vmem, vmem, vmem, vmem,
        ],
        out_specs=(vmem,) * 5,
        scratch_shapes=[
            pltpu.VMEM((tok, feature), half),
            pltpu.VMEM((tok, feature), half),
            pltpu.VMEM((tok, HEAD_DIM), full),
            pltpu.VMEM((tok, HEAD_DIM), full),
            pltpu.VMEM((tok, LANES), full),
            pltpu.VMEM((tok, LANES), full),
            pltpu.VMEM((chunks, 2, 4, capacity, HEAD_DIM), half),
            pltpu.VMEM((chunks, 2, 4, capacity, HEAD_DIM), half),
            pltpu.VMEM((chunks, 2, 4, capacity, HEAD_DIM), half),
            pltpu.VMEM((chunks, 2, 4, capacity, HEAD_DIM), half),
            pltpu.VMEM((heads, n // GROUPS, 2, tok, HEAD_DIM), half),
            pltpu.VMEM((heads, 4, padded, HEAD_DIM), half),
            pltpu.VMEM((heads, 4, window, HEAD_DIM), half),
            pltpu.VMEM((padded, HEAD_DIM), full),
            pltpu.VMEM((padded, HEAD_DIM), full),
            pltpu.VMEM((tok, LANES), full),
            pltpu.VMEM((tok, LANES), full),
            pltpu.VMEM((n,) + gain_rows, full),
            pltpu.VMEM((n, n // replicas) + gain_rows, full),
            pltpu.VMEM((n // replicas,) + gain_rows, full),
            pltpu.VMEM((replicas, n // replicas) + gain_rows, full),
            pltpu.VMEM((n // replicas,) + gain_rows, full),
            pltpu.SemaphoreType.DMA((2,)),
            pltpu.SemaphoreType.DMA((heads,)),
            pltpu.SemaphoreType.DMA((heads,)),
            pltpu.SemaphoreType.DMA((heads,)),
            pltpu.SemaphoreType.DMA((heads,)),
            pltpu.SemaphoreType.DMA((heads,)),
            pltpu.SemaphoreType.DMA((heads,)),
            pltpu.SemaphoreType.DMA((heads,)),
            pltpu.SemaphoreType.DMA((3,)),
            pltpu.SemaphoreType.DMA((3,)),
            pltpu.SemaphoreType.DMA((2, chunks)),
            pltpu.SemaphoreType.DMA((2, chunks)),
            pltpu.SemaphoreType.DMA((2, chunks)),
            pltpu.SemaphoreType.DMA((2, chunks)),
        ],
        compiler_params=pltpu.CompilerParams(
            collective_id=0, has_side_effects=True, vmem_limit_bytes=56 * 1024 * 1024
        ),
    )(
        lengths, q_raw[0], k_raw[0], values[0], grad_out[0],
        q_gain[None], k_gain[None], positions[0][:, None], jnp.asarray(rope_constants(HEAD_DIM)),
    )
    attended, grad_q, grad_k, grad_v, gain_q, gain_k = pl.pallas_call(
        finish,
        out_shape=(jax.ShapeDtypeStruct((tok, feature), half),) * 4
        + (jax.ShapeDtypeStruct((1, feature), full),) * 2,
        in_specs=[vmem] * 5,
        out_specs=(hbm,) * 4 + (vmem,) * 2,
        scratch_shapes=[pltpu.SemaphoreType.DMA((4,))],
        compiler_params=pltpu.CompilerParams(vmem_limit_bytes=6 * 1024 * 1024),
    )(gains, *outs)
    return (
        attended[None], grad_q[None], grad_k[None], grad_v[None], gain_q[0], gain_k[0],
    )


def solution(mesh):
    tokens = P("dp", "seq", None)
    return jax.shard_map(
        on_device,
        mesh=mesh,
        in_specs=(tokens, tokens, tokens, tokens, P(), P(), P("dp", None), P("dp", None, "seq")),
        out_specs=(tokens, tokens, tokens, tokens, P(), P()),
        check_vma=False,
    )
```

```python
import functools
import random

import jax
import jax.numpy as jnp
import numpy as np
from jax import lax
from jax.experimental import pallas as pl
from jax.experimental.pallas import tpu as pltpu
from jax.sharding import PartitionSpec as P

HEAD_DIM = 128
LANES = 128
QUERY_BLOCK = 256
WHOLE_SCORES = 1 << 19
LOG2_E = float(np.log2(np.e))
GROUPS = 4
CHUNK = 2
TILE = 16
ATTEND_LAG = 2
DISTRIBUTE_LAG = 2
NORM_LAG = 1
DEFERRED = 2
AHEAD = 1
EPSILON = 1e-06
MESH = pl.DeviceIdType.MESH


def rope_constants(head_dim):
    half = head_dim // 2
    sixth = head_dim // 6
    first = half - 2 * sixth
    pairs = np.arange(head_dim) % half
    section = (pairs >= first).astype(np.int32) + (pairs >= first + sixth).astype(np.int32)
    begin = np.where(section == 0, 0, np.where(section == 1, first, first + sixth))
    number = np.where(section == 0, first, sixth)
    freqs = (10000.0 ** (-(pairs - begin) / number)).astype(np.float32)
    return (section == np.arange(3)[:, None]).astype(np.float32) * freqs


def needed_modes(longest, rows, heads):
    own = rows // TILE
    total = heads
    while True:
        size = {n: min(own, total // n) for n in range(1, heads + 1)}
        modes, below = [(heads, size[heads], 0)], size[heads] * TILE + 1
        while below <= rows and longest - below > size[heads] * TILE:
            found = [
                (size[n], n) for n in range(1, heads) if size[heads - n] * TILE >= longest - below
            ]
            if not found or max(found)[0] * TILE < below:
                break
            up, count = max(found)
            modes.append((count, up, size[heads - count]))
            below = up * TILE + 1
        else:
            if longest - rows - 1 <= size[heads] * TILE:
                return total, modes + [(0, 0, size[heads])]
        total += 1


def messages(ranks, modes, pairs, base):
    width = len(ranks) // pairs
    tables = {True: [], False: []}
    for upward in tables:
        for count, up, down in modes:
            queue, sent = [], []
            for pair in range(pairs):
                for head in range(pair * width, (pair + 1) * width):
                    if (ranks[head] < count) == upward:
                        queue += [(head, tile) for tile in range(up if upward else down)]
                room = base if pair < pairs - 1 else len(queue)
                sent.append(queue[:room])
                queue = queue[room:]
            tables[upward].append(sent)
    return tables


def ranked(modes, heads, pairs, base):
    rng = random.Random(0)
    width = heads // pairs

    def cost(ranks):
        worst = late = 0
        for count, up, down in modes:
            for upward, size in ((True, up), (False, down)):
                left = 0
                for pair in range(pairs):
                    held = ranks[pair * width:(pair + 1) * width]
                    left += size * sum((rank < count) == upward for rank in held)
                    if pair < pairs - 1:
                        left = max(0, left - base)
                        late += left
                worst = max(worst, left)
        return worst, late

    best = None
    for _ in range(20):
        ranks = list(range(heads))
        rng.shuffle(ranks)
        now, stall = cost(ranks), 0
        while stall < 150:
            i, j = rng.randrange(heads), rng.randrange(heads)
            ranks[i], ranks[j] = ranks[j], ranks[i]
            new = cost(ranks)
            if new <= now:
                stall = 0 if new < now else stall + 1
                now = new
            else:
                ranks[i], ranks[j] = ranks[j], ranks[i]
                stall += 1
        if best is None or now < best[0]:
            best = (now, list(ranks))
    return best[1]


class Plan:
    def __init__(self, longest, rows, heads, pairs):
        self.pairs, self.width = pairs, heads // pairs
        total, self.modes = needed_modes(longest, rows, heads)
        base = -(-total // pairs)
        ranks = ranked(self.modes, heads, pairs, base)
        self.tables = messages(ranks, self.modes, pairs, base)
        last = max(len(sent[-1]) for sents in self.tables.values() for sent in sents)
        self.length = [base] * (pairs - 1) + [last]
        self.begin = [base * pair for pair in range(pairs)]
        self.tiles = base * (pairs - 1) + last
        self.spot, self.until = {}, {}
        for upward, sents in self.tables.items():
            self.until[upward] = [0] * pairs
            for mode, sent in enumerate(sents):
                for number, tiles in enumerate(sent):
                    for place, (head, tile) in enumerate(tiles):
                        self.spot[upward, mode, head, tile] = self.begin[number] + place
                        pair = head // self.width
                        self.until[upward][pair] = max(self.until[upward][pair], number)
            for pair in range(1, pairs):
                self.until[upward][pair] = max(self.until[upward][pair - 1:pair + 1])
            self.until[upward][-1] = pairs - 1
        self.low = [max(up for count, up, _ in self.modes if rank < count) * TILE for rank in ranks]
        self.high = [max(dn for count, _, dn in self.modes if rank >= count) * TILE for rank in ranks]
        self.window = rows + max(low + high for low, high in zip(self.low, self.high))
        self.padded = -(-self.window // LANES) * LANES
        self.span = max(3 * rows, rows - min(self.low) + self.padded)


def dot(left, right, left_dim, right_dim):
    return lax.dot_general(
        left, right, (((left_dim,), (right_dim,)), ((), ())), preferred_element_type=jnp.float32
    )


def kernel(
    sizes,
    len_ref, q_hbm, k_hbm, v_ref, do_ref, gq_ref, gk_ref, pos_ref, freq_ref,
    att_ref, dq_ref, dk_ref, dv_ref, gain_ref,
    q_ref, k_ref, cos_ref, sin_ref, inner_q, inner_k,
    give, take, give_back, take_back, sent, recv, back, key_acc, value_acc, scale_q, scale_k,
    part, seq_part, dp_sum, dp_part, total,
    raw_sem, in_send, in_recv, own_sem, out_send, out_recv, late_send, late_recv,
    gain_send, gain_recv,
    halo_send, halo_recv, beside_send, beside_recv,
):
    n, replicas, heads, tok, clips, reach, plan = sizes
    members = n // GROUPS
    group_tokens = members * tok
    chunks = heads // CHUNK
    window, padded = plan.window, plan.padded
    feature = members * heads * HEAD_DIM
    ratio = GROUPS
    shared = heads // ratio
    me = lax.axis_index("seq")
    side = me // members
    place_in = lax.rem(me, members)
    my_dp = lax.axis_index("dp")
    scale = HEAD_DIM ** (-0.5)

    def peer(step):
        return lax.rem(me + step, n)

    def member(step):
        return lax.rem(place_in + step, members)

    def device(group, index):
        return (my_dp, group * members + index)

    def columns(owner, head):
        return pl.ds(pl.multiple_of((owner * heads + head) * HEAD_DIM, HEAD_DIM), HEAD_DIM)

    def rows(owner):
        return pl.ds(pl.multiple_of(group_tokens + owner * tok, TILE), tok)

    def each_side(act):
        @pl.when(side > 0)
        def _():
            act(0, side - 1)

        @pl.when(side < GROUPS - 1)
        def _():
            act(1, side + 1)

    def remote(src, dst, send_sem, recv_sem, device):
        return pltpu.make_async_remote_copy(
            src_ref=src, dst_ref=dst, send_sem=send_sem, recv_sem=recv_sem,
            device_id=device, device_id_type=MESH,
        )

    loads = [
        pltpu.make_async_copy(q_hbm, q_ref, raw_sem.at[0]),
        pltpu.make_async_copy(k_hbm, k_ref, raw_sem.at[1]),
    ]
    for load in loads:
        load.start()

    barrier = pltpu.get_barrier_semaphore()
    for step in range(1, n):
        pl.semaphore_signal(barrier, inc=1, device_id=(my_dp, peer(step)), device_id_type=MESH)
    for step in range(1, replicas):
        other = lax.rem(my_dp + step, replicas)
        pl.semaphore_signal(barrier, inc=1, device_id=(other, me), device_id_type=MESH)
    pl.semaphore_wait(barrier, n - 1 + replicas - 1)

    def send_values(head):
        cols = columns(place_in, head)
        for place, ref in ((2, v_ref), (3, do_ref)):
            pltpu.make_async_copy(
                ref.at[:, cols], recv.at[head, place, rows(place_in), :], own_sem.at[head]
            ).start()

        @pl.loop(1, members)
        def _(step):
            other = member(step)
            for place, ref in ((2, v_ref), (3, do_ref)):
                remote(
                    ref.at[:, columns(other, head)], recv.at[head, place, rows(place_in), :],
                    in_send.at[head], in_recv.at[head], device(side, other),
                ).start()

    ahead = min(AHEAD, chunks)
    for head in range(ahead * CHUNK):
        send_values(head)

    held = jnp.concatenate([pos_ref[axis] for axis in range(3)], axis=0)
    angle = lax.dot_general(
        held.astype(jnp.float32), freq_ref[...], (((0,), (0,)), ((), ())),
        precision=lax.Precision.HIGHEST, preferred_element_type=jnp.float32,
    )
    negative = lax.broadcasted_iota(jnp.int32, (tok, HEAD_DIM), 1) < HEAD_DIM // 2
    cos_ref[...] = jnp.cos(angle)
    sine = jnp.sin(angle)
    sin_ref[...] = jnp.where(negative, -sine, sine)
    for load in loads:
        load.wait()

    def squares(index, sums):
        cols = pl.ds(pl.multiple_of(index * LANES, LANES), LANES)
        query = q_ref[:, cols].astype(jnp.float32)
        keys = k_ref[:, cols].astype(jnp.float32)
        return sums[0] + query * query, sums[1] + keys * keys

    zero = jnp.zeros((tok, LANES), jnp.float32)
    sum_q, sum_k = lax.fori_loop(0, feature // LANES, squares, (zero, zero))
    for sums, target in ((sum_q, scale_q), (sum_k, scale_k)):
        mean = jnp.sum(sums, axis=1, keepdims=True) / feature
        target[...] = jnp.broadcast_to(lax.rsqrt(mean + EPSILON), (tok, LANES))

    def rotated(ref, gain, norm, cols):
        x = ref[:, cols].astype(jnp.float32) * norm[...] * gain[:, cols]
        turned = x * cos_ref[...] + pltpu.roll(x, HEAD_DIM // 2, 1) * sin_ref[...]
        return turned.astype(jnp.bfloat16)

    @pl.loop(0, chunks)
    def _(chunk):
        for index in range(CHUNK):
            head = chunk * CHUNK + index

            @pl.loop(1, members)
            def _(step):
                other = member(step)
                cols = columns(other, head)
                sent[head, other, 0] = rotated(q_ref, gq_ref, scale_q, cols)
                sent[head, other, 1] = rotated(k_ref, gk_ref, scale_k, cols)
                remote(
                    sent.at[head, other], recv.at[head, 0:2, rows(place_in), :],
                    in_send.at[head], in_recv.at[head], device(side, other),
                ).start()

            cols = columns(place_in, head)
            for place, (ref, gain, norm) in enumerate(
                ((q_ref, gq_ref, scale_q), (k_ref, gk_ref, scale_k))
            ):
                recv[head, place, rows(place_in), :] = rotated(ref, gain, norm, cols)

        @pl.when(chunk + ahead < chunks)
        def _():
            for index in range(CHUNK):
                send_values((chunk + ahead) * CHUNK + index)

    bounds = []
    running = len_ref[0, 0]
    for clip in range(clips):
        bounds.append(running)
        if clip + 1 < clips:
            running = running + len_ref[0, clip + 1]

    def straddle(middle):
        first, last = jnp.int32(0), jnp.int32(n * tok)
        for bound in bounds:
            first = jnp.maximum(first, jnp.where(bound <= middle, bound, 0))
            last = jnp.minimum(last, jnp.where(bound > middle, bound, n * tok))
        below, above = middle - first, last - middle
        mode = jnp.int32(len(plan.modes) - 1)
        for number in reversed(range(len(plan.modes) - 1)):
            count, up, down = plan.modes[number]
            fits = below <= up * TILE
            if count < heads:
                fits = fits & (above <= down * TILE)
            mode = jnp.where(fits, number, mode)
        return first, last, mode

    token_start = side * group_tokens
    straddles = straddle(token_start), straddle(token_start + group_tokens)

    def clear(begin, end):
        @pl.loop(0, heads)
        def _(head):
            recv[head, :, begin:end, :] = jnp.zeros((4, end - begin, HEAD_DIM), jnp.bfloat16)

    clear(2 * group_tokens, plan.span)

    @pl.when(side == 0)
    def _():
        clear(0, group_tokens)

    def segment(shape, dim, start, shift):
        inside = lax.broadcasted_iota(jnp.int32, shape, dim) + start
        places = inside + (token_start - shift)
        found = jnp.zeros(shape, jnp.int32)
        for bound in bounds:
            found = found + (places >= bound).astype(jnp.int32)
        valid = (inside < window) & (places >= 0) & (places < n * tok)
        return jnp.where(valid, found, -1)

    def masks_of(which):
        held = jnp.full((TILE, HEAD_DIM), straddles[which][2], jnp.int32)
        return [held == mode for mode in range(len(plan.modes))]

    def row_of(upward, mode, tile):
        return (group_tokens if upward else 0) + (tile - (plan.modes[mode][1] if upward else 0)) * TILE

    def select(choices, masks):
        (value, _), *others = choices
        for other, modes in others:
            for mode in modes:
                value = jnp.where(masks[mode], other, value)
        return value

    def gather(target, source, which, upward, region, pair):
        masks = masks_of(which)

        @pl.loop(0, 4)
        def _(place):
            for spot in range(plan.length[pair]):
                wanted = {}
                for mode, sent in enumerate(plan.tables[upward]):
                    if spot < len(sent[pair]):
                        head, tile = sent[pair][spot]
                        wanted.setdefault((head, row_of(upward, mode, tile)), []).append(mode)
                ordered = sorted(wanted.items(), key=lambda item: -len(item[1]))
                choices = [
                    (source[head, place, region + row:region + row + TILE, :], modes)
                    for (head, row), modes in ordered
                ]
                start = (plan.begin[pair] + spot) * TILE
                target[which, place, start:start + TILE, :] = select(choices, masks)

    def scatter(source, target, which, upward, region, pair, merged):
        masks = masks_of(which)
        first, last, mode_now = straddles[which]
        lane_rows = lax.broadcasted_iota(jnp.int32, (TILE, HEAD_DIM), 0)
        limits = []
        for mode in range(len(plan.modes)):
            if upward:
                limits.append(jnp.where(mode_now == mode, first, n * tok))
            else:
                limits.append(jnp.where(mode_now == mode, last, -1))

        @pl.loop(0, 4)
        def _(place):
            for head in range(pair * plan.width, (pair + 1) * plan.width):
                wanted = {}
                for mode, (_, up, down) in enumerate(plan.modes):
                    for tile in range(up if upward else down):
                        spot = plan.spot.get((upward, mode, head, tile))
                        if spot is not None:
                            row = row_of(upward, mode, tile)
                            wanted.setdefault(row, {}).setdefault(spot, []).append(mode)
                for row, spots in wanted.items():
                    ordered = sorted(spots.items(), key=lambda item: -len(item[1]))
                    choices = [
                        (source[which, place, spot * TILE:(spot + 1) * TILE, :], modes)
                        for spot, modes in ordered
                    ]
                    here = region + row
                    if merged:
                        tokens = lane_rows + (token_start + row)
                        inside = [tokens >= limit if upward else tokens < limit for limit in limits]
                        own = target[head, place, here:here + TILE, :]
                        value = select([(own, [])] + choices, inside)
                    else:
                        value = select(choices, masks)
                    target[head, place, here:here + TILE, :] = value

    def part_of(ref, which, pair):
        return ref.at[which, :, pl.ds(plan.begin[pair] * TILE, plan.length[pair] * TILE), :]

    def wait_messages(ref, sem, which, upward, pair):
        begin = plan.until[upward][pair - 1] + 1 if pair else 0
        for number in range(begin, plan.until[upward][pair] + 1):
            held = part_of(ref, which, number)
            pltpu.make_async_copy(held, held, sem.at[which, number]).wait()

    def relay(pair):
        for head in range(pair * plan.width, (pair + 1) * plan.width):
            arrived = recv.at[head, :, pl.ds(0, (members - 1) * tok), :]
            pltpu.make_async_copy(arrived, arrived, in_recv.at[head]).wait()
            own = recv.at[head, pl.ds(2, 2), pl.ds(0, tok), :]
            pltpu.make_async_copy(own, own, own_sem.at[head]).wait()

        def act(which, group):
            gather(give, recv, which, which == 1, group_tokens, pair)
            remote(
                part_of(give, which, pair), part_of(take, 1 - which, pair),
                halo_send.at[which, pair], halo_recv.at[1 - which, pair], device(group, place_in),
            ).start()

        each_side(act)

    def arrive(pair):
        def act(which, group):
            upward = which == 0
            wait_messages(take, halo_recv, which, upward, pair)
            scatter(take, recv, which, upward, 0 if upward else 2 * group_tokens, pair, False)

        each_side(act)

    def attend(chunk):
        @pl.loop(0, CHUNK)
        def _(index):
            head = chunk * CHUNK + index
            shift = jnp.int32(plan.low[0])
            for other in range(1, heads):
                shift = jnp.where(head == other, plan.low[other], shift)
            attend_head(head, shift)

    def give_results(pair):
        def act(which, group):
            upward = which == 0
            gather(give_back, back, which, upward, 0 if upward else 2 * group_tokens, pair)
            remote(
                part_of(give_back, which, pair), part_of(take_back, 1 - which, pair),
                beside_send.at[which, pair], beside_recv.at[1 - which, pair],
                device(group, place_in),
            ).start()

        each_side(act)

    def attend_head(head, shift):
        base = group_tokens - shift

        def at(start, size):
            return pl.ds(pl.multiple_of(base + start, TILE), size)

        whole = window * padded <= WHOLE_SCORES
        step_rows = window if whole else QUERY_BLOCK
        if not whole:
            key_acc[...] = jnp.zeros_like(key_acc)
            value_acc[...] = jnp.zeros_like(value_acc)
        for start in range(0, window, step_rows):
            block = min(step_rows, window - start)
            first = max(0, start - reach) // LANES * LANES
            last = min(padded, -(-(start + block + reach) // LANES) * LANES)
            query = recv[head, 0, at(start, block), :]
            keys = recv[head, 1, at(first, last - first), :]
            value_rows = recv[head, 2, at(first, last - first), :]
            cot = recv[head, 3, at(start, block), :]
            live = segment((block, 1), 0, start, shift) == segment((1, last - first), 1, first, shift)
            scores = jnp.where(live, dot(query, keys, 1, 1), -1e30)
            highest = jnp.max(scores, axis=1, keepdims=True)
            expon = jnp.exp2((scores - highest) * (scale * LOG2_E))
            probs = expon * (1.0 / jnp.sum(expon, axis=1, keepdims=True))
            half = probs.astype(jnp.bfloat16)
            context = dot(half, value_rows, 1, 0).astype(jnp.bfloat16)
            delta = jnp.sum(
                cot.astype(jnp.float32) * context.astype(jnp.float32), axis=1, keepdims=True
            )
            dprob = dot(cot, value_rows, 1, 1)
            dscore = (probs * (dprob - delta)).astype(jnp.bfloat16)
            back[head, 2, at(start, block), :] = context
            back[head, 0, at(start, block), :] = (dot(dscore, keys, 1, 0) * scale).astype(jnp.bfloat16)
            key_part = (dot(query, dscore, 0, 0) * scale).T
            value_part = dot(cot, half, 0, 0).T
            if whole:
                back[head, 1, at(0, window), :] = key_part[0:window].astype(jnp.bfloat16)
                back[head, 3, at(0, window), :] = value_part[0:window].astype(jnp.bfloat16)
            else:
                key_acc[first:last, :] += key_part
                value_acc[first:last, :] += value_part
        if not whole:
            back[head, 1, at(0, window), :] = key_acc[0:window, :].astype(jnp.bfloat16)
            back[head, 3, at(0, window), :] = value_acc[0:window, :].astype(jnp.bfloat16)

    def merge(pair):
        def act(which, group):
            upward = which == 1
            wait_messages(take_back, beside_recv, which, upward, pair)
            scatter(take_back, back, which, upward, group_tokens, pair, True)

        each_side(act)

    def distribute(chunk):
        outward(chunk, 0, (dq_ref, dk_ref), out_send, out_recv)

        @pl.when(chunk < chunks - DEFERRED)
        def _():
            outward(chunk, 2, (att_ref, dv_ref), late_send, late_recv)

    def outward(chunk, first, targets, send, receive):
        for index in range(CHUNK):
            head = chunk * CHUNK + index
            cols = columns(place_in, head)

            @pl.loop(1, members)
            def _(step):
                other = member(step)
                for place, target in enumerate(targets):
                    remote(
                        back.at[head, first + place, rows(other), :], target.at[:, cols],
                        send.at[head], receive.at[head], device(side, other),
                    ).start()

            for place, target in enumerate(targets):
                target[:, cols] = back[head, first + place, rows(place_in), :]

    def arrived_pair(head, sem):
        held = recv.at[head, 0:2, pl.ds(0, (members - 1) * tok), :]
        pltpu.make_async_copy(held, held, sem.at[head]).wait()

    def turned_back(grad, ref, norm, cols):
        grads = grad[:, cols].astype(jnp.float32)
        turned = grads * cos_ref[...] - pltpu.roll(grads, HEAD_DIM // 2, 1) * sin_ref[...]
        return turned, ref[:, cols].astype(jnp.float32) * norm[...]

    sides = (
        (dq_ref, q_ref, gq_ref, scale_q, inner_q), (dk_ref, k_ref, gk_ref, scale_k, inner_k),
    )
    inner_q[...] = zero
    inner_k[...] = zero

    def first_pass(chunk):
        for index in range(CHUNK):
            head = chunk * CHUNK + index
            arrived_pair(head, out_recv)

            @pl.loop(0, members)
            def _(owner):
                cols = columns(owner, head)
                for place, (grad, ref, gain, norm, inner) in enumerate(sides):
                    turned, hat = turned_back(grad, ref, norm, cols)
                    both = turned * hat
                    row = place * shared + lax.rem(head, shared)
                    part[owner * ratio + head // shared, pl.ds(row, 1), :] = jnp.sum(
                        both, axis=0, keepdims=True
                    )
                    inner[...] += both * gain[:, cols]

    @pl.loop(0, chunks + ATTEND_LAG + DISTRIBUTE_LAG + NORM_LAG)
    def _(step):
        def each_pair(now, act):
            for pair in range(chunks):
                @pl.when(now == pair)
                def _():
                    act(pair)

        each_pair(step, relay)
        attended = step - ATTEND_LAG
        each_pair(attended, arrive)

        @pl.when((attended >= 0) & (attended < chunks))
        def _():
            attend(attended)

        each_pair(attended, give_results)
        merged = attended - DISTRIBUTE_LAG
        each_pair(merged, merge)

        @pl.when((merged >= 0) & (merged < chunks))
        def _():
            distribute(merged)

        @pl.when(step >= ATTEND_LAG + DISTRIBUTE_LAG + NORM_LAG)
        def _():
            first_pass(step - ATTEND_LAG - DISTRIBUTE_LAG - NORM_LAG)

    per = n // replicas

    def portion(index):
        return pl.ds(index * per, per)

    for step in range(1, replicas):
        other = lax.rem(my_dp + step, replicas)
        remote(
            part.at[portion(other)], dp_part.at[my_dp], gain_send.at[0], gain_recv.at[0], (other, me)
        ).start()
    dp_part[my_dp] = part[portion(my_dp)]

    @pl.loop(chunks - min(DEFERRED, chunks), chunks)
    def _(chunk):
        outward(chunk, 2, (att_ref, dv_ref), late_send, late_recv)

    means = [
        jnp.broadcast_to(jnp.sum(inner[...], axis=1, keepdims=True) / feature, (tok, LANES))
        for inner in (inner_q, inner_k)
    ]

    def second_pass(index):
        cols = pl.ds(pl.multiple_of(index * LANES, LANES), LANES)
        for (grad, ref, gain, norm, _), mean in zip(sides, means):
            turned, hat = turned_back(grad, ref, norm, cols)
            result = norm[...] * (turned * gain[:, cols] - hat * mean)
            grad[:, cols] = result.astype(jnp.bfloat16)

    pl.loop(0, feature // LANES)(second_pass)

    def wait_all(ref, count, sem):
        held = ref.at[pl.ds(0, count)]
        pltpu.make_async_copy(held, held, sem).wait()

    wait_all(dp_part, replicas - 1, gain_recv.at[0])
    dp_sum[...] = jnp.sum(dp_part[...], axis=0)

    @pl.loop(1, n)
    def _(step):
        other = peer(step)
        remote(
            dp_sum, seq_part.at[me], gain_send.at[1], gain_recv.at[1], (my_dp, other)
        ).start()

    seq_part[me] = dp_sum[...]
    wait_all(seq_part, n - 1, gain_recv.at[1])
    total[...] = jnp.sum(seq_part[...], axis=0) / replicas
    for step in range(1, replicas):
        other = lax.rem(my_dp + step, replicas)
        remote(
            total, gain_ref.at[portion(my_dp)], gain_send.at[2], gain_recv.at[2], (other, me)
        ).start()
    gain_ref[portion(my_dp)] = total[...]
    wait_all(dp_part, replicas - 1, gain_recv.at[2])

    wait_all(dp_part, replicas - 1, gain_send.at[0])
    wait_all(seq_part, n - 1, gain_send.at[1])
    wait_all(dp_part, replicas - 1, gain_send.at[2])

    @pl.loop(0, heads)
    def _(head):
        moved = recv.at[head, :, pl.ds(0, (members - 1) * tok), :]
        pltpu.make_async_copy(moved, moved, in_send.at[head]).wait()
        arrived_pair(head, out_send)
        arrived_pair(head, late_send)
        arrived_pair(head, late_recv)

    for pair in range(chunks):
        def drain(which, group):
            held = part_of(give, which, pair)
            pltpu.make_async_copy(held, held, halo_send.at[which, pair]).wait()
            pltpu.make_async_copy(held, held, beside_send.at[which, pair]).wait()

        each_side(drain)


def finish(gains_ref, *refs):
    arrays, targets, (gq_ref, gk_ref), sems = refs[:4], refs[4:8], refs[8:10], refs[10]
    copies = [
        pltpu.make_async_copy(source, target, sems.at[index])
        for index, (source, target) in enumerate(zip(arrays, targets))
    ]
    for copy in copies:
        copy.start()
    owners, shared = gains_ref.shape[0], gains_ref.shape[1] // 2
    for owner in range(owners):
        for row in range(shared):
            cols = slice((owner * shared + row) * LANES, (owner * shared + row + 1) * LANES)
            gq_ref[:, cols] = gains_ref[owner, row:row + 1, :]
            gk_ref[:, cols] = gains_ref[owner, shared + row:shared + row + 1, :]
    for copy in copies:
        copy.wait()


def on_device(q_raw, k_raw, values, grad_out, q_gain, k_gain, lengths, positions):
    n = lax.axis_size("seq")
    replicas = lax.axis_size("dp")
    tok, feature = q_raw.shape[1:]
    shared = feature // n // HEAD_DIM
    heads = GROUPS * shared
    tokens = n * tok
    reach = tokens // 3 - 1
    group_tokens = tokens // GROUPS
    chunks = heads // CHUNK
    plan = Plan(reach + 1, group_tokens, heads, chunks)
    sizes = (n, replicas, heads, tok, lengths.shape[1], reach, plan)
    vmem = pl.BlockSpec(memory_space=pltpu.VMEM)
    hbm = pl.BlockSpec(memory_space=pl.ANY)
    gain_rows = (2 * shared, LANES)
    half, full = jnp.bfloat16, jnp.float32
    *outs, gains = pl.pallas_call(
        functools.partial(kernel, sizes),
        out_shape=(
            *[pltpu.VMEM((tok, feature), half)] * 4,
            pltpu.VMEM((n,) + gain_rows, full),
        ),
        in_specs=[
            pl.BlockSpec(memory_space=pltpu.SMEM), hbm, hbm, hbm, hbm, vmem, vmem, vmem, vmem,
        ],
        out_specs=(vmem,) * 5,
        scratch_shapes=[
            pltpu.VMEM((tok, feature), half),
            pltpu.VMEM((tok, feature), half),
            pltpu.VMEM((tok, HEAD_DIM), full),
            pltpu.VMEM((tok, HEAD_DIM), full),
            pltpu.VMEM((tok, LANES), full),
            pltpu.VMEM((tok, LANES), full),
            pltpu.VMEM((2, 4, plan.tiles * TILE, HEAD_DIM), half),
            pltpu.VMEM((2, 4, plan.tiles * TILE, HEAD_DIM), half),
            pltpu.VMEM((2, 4, plan.tiles * TILE, HEAD_DIM), half),
            pltpu.VMEM((2, 4, plan.tiles * TILE, HEAD_DIM), half),
            pltpu.VMEM((heads, n // GROUPS, 2, tok, HEAD_DIM), half),
            pltpu.VMEM((heads, 4, plan.span, HEAD_DIM), half),
            pltpu.VMEM((heads, 4, plan.span, HEAD_DIM), half),
            pltpu.VMEM((plan.padded, HEAD_DIM), full),
            pltpu.VMEM((plan.padded, HEAD_DIM), full),
            pltpu.VMEM((tok, LANES), full),
            pltpu.VMEM((tok, LANES), full),
            pltpu.VMEM((n,) + gain_rows, full),
            pltpu.VMEM((n, n // replicas) + gain_rows, full),
            pltpu.VMEM((n // replicas,) + gain_rows, full),
            pltpu.VMEM((replicas, n // replicas) + gain_rows, full),
            pltpu.VMEM((n // replicas,) + gain_rows, full),
            pltpu.SemaphoreType.DMA((2,)),
            pltpu.SemaphoreType.DMA((heads,)),
            pltpu.SemaphoreType.DMA((heads,)),
            pltpu.SemaphoreType.DMA((heads,)),
            pltpu.SemaphoreType.DMA((heads,)),
            pltpu.SemaphoreType.DMA((heads,)),
            pltpu.SemaphoreType.DMA((heads,)),
            pltpu.SemaphoreType.DMA((heads,)),
            pltpu.SemaphoreType.DMA((3,)),
            pltpu.SemaphoreType.DMA((3,)),
            pltpu.SemaphoreType.DMA((2, chunks)),
            pltpu.SemaphoreType.DMA((2, chunks)),
            pltpu.SemaphoreType.DMA((2, chunks)),
            pltpu.SemaphoreType.DMA((2, chunks)),
        ],
        compiler_params=pltpu.CompilerParams(
            collective_id=0, has_side_effects=True, vmem_limit_bytes=56 * 1024 * 1024
        ),
    )(
        lengths, q_raw[0], k_raw[0], values[0], grad_out[0],
        q_gain[None], k_gain[None], positions[0][:, None], jnp.asarray(rope_constants(HEAD_DIM)),
    )
    attended, grad_q, grad_k, grad_v, gain_q, gain_k = pl.pallas_call(
        finish,
        out_shape=(jax.ShapeDtypeStruct((tok, feature), half),) * 4
        + (jax.ShapeDtypeStruct((1, feature), full),) * 2,
        in_specs=[vmem] * 5,
        out_specs=(hbm,) * 4 + (vmem,) * 2,
        scratch_shapes=[pltpu.SemaphoreType.DMA((4,))],
        compiler_params=pltpu.CompilerParams(vmem_limit_bytes=6 * 1024 * 1024),
    )(gains, *outs)
    return (
        attended[None], grad_q[None], grad_k[None], grad_v[None], gain_q[0], gain_k[0],
    )


def solution(mesh):
    tokens = P("dp", "seq", None)
    return jax.shard_map(
        on_device,
        mesh=mesh,
        in_specs=(tokens, tokens, tokens, tokens, P(), P(), P("dp", None), P("dp", None, "seq")),
        out_specs=(tokens, tokens, tokens, tokens, P(), P()),
        check_vma=False,
    )
```

```python
import functools
import random

import jax
import jax.numpy as jnp
import numpy as np
from jax import lax
from jax.experimental import pallas as pl
from jax.experimental.pallas import tpu as pltpu
from jax.sharding import PartitionSpec as P

HEAD_DIM = 128
LANES = 128
QUERY_BLOCK = 256
WHOLE_SCORES = 1 << 19
LOG2_E = float(np.log2(np.e))
GROUPS = 4
CHUNK = 2
TILE = 16
ATTEND_LAG = 2
DISTRIBUTE_LAG = 2
NORM_LAG = 1
DEFERRED = 2
AHEAD = 1
SENT_AHEAD = 8
EPSILON = 1e-06
MESH = pl.DeviceIdType.MESH


def rope_constants(head_dim):
    half = head_dim // 2
    sixth = head_dim // 6
    first = half - 2 * sixth
    pairs = np.arange(head_dim) % half
    section = (pairs >= first).astype(np.int32) + (pairs >= first + sixth).astype(np.int32)
    begin = np.where(section == 0, 0, np.where(section == 1, first, first + sixth))
    number = np.where(section == 0, first, sixth)
    freqs = (10000.0 ** (-(pairs - begin) / number)).astype(np.float32)
    return (section == np.arange(3)[:, None]).astype(np.float32) * freqs


def needed_modes(longest, rows, heads):
    own = rows // TILE
    total = heads
    while True:
        size = {n: min(own, total // n) for n in range(1, heads + 1)}
        modes, below = [(heads, size[heads], 0)], size[heads] * TILE + 1
        while below <= rows and longest - below > size[heads] * TILE:
            found = [
                (size[n], n) for n in range(1, heads) if size[heads - n] * TILE >= longest - below
            ]
            if not found or max(found)[0] * TILE < below:
                break
            up, count = max(found)
            modes.append((count, up, size[heads - count]))
            below = up * TILE + 1
        else:
            if longest - rows - 1 <= size[heads] * TILE:
                return total, modes + [(0, 0, size[heads])]
        total += 1


def messages(ranks, modes, pairs, base):
    width = len(ranks) // pairs
    tables = {True: [], False: []}
    for upward in tables:
        for count, up, down in modes:
            queue, sent = [], []
            for pair in range(pairs):
                for head in range(pair * width, (pair + 1) * width):
                    if (ranks[head] < count) == upward:
                        queue += [(head, tile) for tile in range(up if upward else down)]
                room = base if pair < pairs - 1 else len(queue)
                sent.append(queue[:room])
                queue = queue[room:]
            tables[upward].append(sent)
    return tables


def ranked(modes, heads, pairs, base):
    rng = random.Random(0)
    width = heads // pairs

    def cost(ranks):
        worst = late = 0
        for count, up, down in modes:
            for upward, size in ((True, up), (False, down)):
                left = 0
                for pair in range(pairs):
                    held = ranks[pair * width:(pair + 1) * width]
                    left += size * sum((rank < count) == upward for rank in held)
                    if pair < pairs - 1:
                        left = max(0, left - base)
                        late += left
                worst = max(worst, left)
        return worst, late

    best = None
    for _ in range(20):
        ranks = list(range(heads))
        rng.shuffle(ranks)
        now, stall = cost(ranks), 0
        while stall < 150:
            i, j = rng.randrange(heads), rng.randrange(heads)
            ranks[i], ranks[j] = ranks[j], ranks[i]
            new = cost(ranks)
            if new <= now:
                stall = 0 if new < now else stall + 1
                now = new
            else:
                ranks[i], ranks[j] = ranks[j], ranks[i]
                stall += 1
        if best is None or now < best[0]:
            best = (now, list(ranks))
    return best[1]


class Plan:
    def __init__(self, longest, rows, heads, pairs):
        self.pairs, self.width = pairs, heads // pairs
        total, self.modes = needed_modes(longest, rows, heads)
        base = -(-total // pairs)
        ranks = ranked(self.modes, heads, pairs, base)
        self.tables = messages(ranks, self.modes, pairs, base)
        last = max(len(sent[-1]) for sents in self.tables.values() for sent in sents)
        self.length = [base] * (pairs - 1) + [last]
        self.begin = [base * pair for pair in range(pairs)]
        self.tiles = base * (pairs - 1) + last
        self.spot, self.until = {}, {}
        for upward, sents in self.tables.items():
            self.until[upward] = [0] * pairs
            for mode, sent in enumerate(sents):
                for number, tiles in enumerate(sent):
                    for place, (head, tile) in enumerate(tiles):
                        self.spot[upward, mode, head, tile] = self.begin[number] + place
                        pair = head // self.width
                        self.until[upward][pair] = max(self.until[upward][pair], number)
            for pair in range(1, pairs):
                self.until[upward][pair] = max(self.until[upward][pair - 1:pair + 1])
            self.until[upward][-1] = pairs - 1
        self.low = [max(up for count, up, _ in self.modes if rank < count) * TILE for rank in ranks]
        self.high = [max(dn for count, _, dn in self.modes if rank >= count) * TILE for rank in ranks]
        self.window = rows + max(low + high for low, high in zip(self.low, self.high))
        self.padded = -(-self.window // LANES) * LANES
        self.span = max(3 * rows, rows - min(self.low) + self.padded)


def dot(left, right, left_dim, right_dim):
    return lax.dot_general(
        left, right, (((left_dim,), (right_dim,)), ((), ())), preferred_element_type=jnp.float32
    )


def kernel(
    sizes,
    len_ref, q_hbm, k_hbm, v_ref, do_ref, gq_ref, gk_ref, pos_ref, freq_ref,
    att_ref, dq_ref, dk_ref, dv_ref, gain_ref,
    q_ref, k_ref, cos_ref, sin_ref, inner_q, inner_k,
    give, take, give_back, take_back, sent, recv, back, key_acc, value_acc, scale_q, scale_k,
    part, seq_part, dp_sum, dp_part, total,
    raw_sem, in_send, in_recv, own_sem, out_send, out_recv, late_send, late_recv,
    gain_send, gain_recv,
    halo_send, halo_recv, beside_send, beside_recv,
):
    n, replicas, heads, tok, clips, reach, plan = sizes
    members = n // GROUPS
    group_tokens = members * tok
    chunks = heads // CHUNK
    window, padded = plan.window, plan.padded
    feature = members * heads * HEAD_DIM
    ratio = GROUPS
    shared = heads // ratio
    me = lax.axis_index("seq")
    side = me // members
    place_in = lax.rem(me, members)
    my_dp = lax.axis_index("dp")
    scale = HEAD_DIM ** (-0.5)

    def peer(step):
        return lax.rem(me + step, n)

    def member(step):
        return lax.rem(place_in + step, members)

    def device(group, index):
        return (my_dp, group * members + index)

    def columns(owner, head):
        return pl.ds(pl.multiple_of((owner * heads + head) * HEAD_DIM, HEAD_DIM), HEAD_DIM)

    def rows(owner):
        return pl.ds(pl.multiple_of(group_tokens + owner * tok, TILE), tok)

    def each_side(act):
        @pl.when(side > 0)
        def _():
            act(0, side - 1)

        @pl.when(side < GROUPS - 1)
        def _():
            act(1, side + 1)

    def remote(src, dst, send_sem, recv_sem, device):
        return pltpu.make_async_remote_copy(
            src_ref=src, dst_ref=dst, send_sem=send_sem, recv_sem=recv_sem,
            device_id=device, device_id_type=MESH,
        )

    loads = [
        pltpu.make_async_copy(q_hbm, q_ref, raw_sem.at[0]),
        pltpu.make_async_copy(k_hbm, k_ref, raw_sem.at[1]),
    ]
    for load in loads:
        load.start()

    barrier = pltpu.get_barrier_semaphore()

    def greet(target):
        pl.semaphore_signal(barrier, inc=1, device_id=target, device_id_type=MESH)

    for step in range(1, members):
        greet(device(side, member(step)))
    for step in range(1, replicas):
        greet((lax.rem(my_dp + step, replicas), me))
    each_side(lambda which, group: greet(device(group, place_in)))
    sides_here = jnp.minimum(side, 1) + jnp.minimum(GROUPS - 1 - side, 1)
    pl.semaphore_wait(barrier, members - 1 + replicas - 1 + sides_here)

    def send_values(head):
        cols = columns(place_in, head)
        for place, ref in ((2, v_ref), (3, do_ref)):
            pltpu.make_async_copy(
                ref.at[:, cols], recv.at[head, place, rows(place_in), :], own_sem.at[head]
            ).start()

        @pl.loop(1, members)
        def _(step):
            other = member(step)
            for place, ref in ((2, v_ref), (3, do_ref)):
                remote(
                    ref.at[:, columns(other, head)], recv.at[head, place, rows(place_in), :],
                    in_send.at[0], in_recv.at[head], device(side, other),
                ).start()

    ahead = min(AHEAD, chunks)
    for head in range(ahead * CHUNK):
        send_values(head)

    held = jnp.concatenate([pos_ref[axis] for axis in range(3)], axis=0)
    angle = lax.dot_general(
        held.astype(jnp.float32), freq_ref[...], (((0,), (0,)), ((), ())),
        precision=lax.Precision.HIGHEST, preferred_element_type=jnp.float32,
    )
    negative = lax.broadcasted_iota(jnp.int32, (tok, HEAD_DIM), 1) < HEAD_DIM // 2
    cos_ref[...] = jnp.cos(angle)
    sine = jnp.sin(angle)
    sin_ref[...] = jnp.where(negative, -sine, sine)
    for load in loads:
        load.wait()

    def squares(index, sums):
        cols = pl.ds(pl.multiple_of(index * LANES, LANES), LANES)
        query = q_ref[:, cols].astype(jnp.float32)
        keys = k_ref[:, cols].astype(jnp.float32)
        return sums[0] + query * query, sums[1] + keys * keys

    zero = jnp.zeros((tok, LANES), jnp.float32)
    sum_q, sum_k = lax.fori_loop(0, feature // LANES, squares, (zero, zero))
    for sums, target in ((sum_q, scale_q), (sum_k, scale_k)):
        mean = jnp.sum(sums, axis=1, keepdims=True) / feature
        target[...] = jnp.broadcast_to(lax.rsqrt(mean + EPSILON), (tok, LANES))

    def rotated(ref, gain, norm, cols):
        x = ref[:, cols].astype(jnp.float32) * norm[...] * gain[:, cols]
        turned = x * cos_ref[...] + pltpu.roll(x, HEAD_DIM // 2, 1) * sin_ref[...]
        return turned.astype(jnp.bfloat16)

    def send_pair(chunk):
        for index in range(CHUNK):
            head = chunk * CHUNK + index

            @pl.loop(1, members)
            def _(step):
                other = member(step)
                cols = columns(other, head)
                sent[head, other, 0] = rotated(q_ref, gq_ref, scale_q, cols)
                sent[head, other, 1] = rotated(k_ref, gk_ref, scale_k, cols)
                remote(
                    sent.at[head, other], recv.at[head, 0:2, rows(place_in), :],
                    in_send.at[0], in_recv.at[head], device(side, other),
                ).start()

            cols = columns(place_in, head)
            for place, (ref, gain, norm) in enumerate(
                ((q_ref, gq_ref, scale_q), (k_ref, gk_ref, scale_k))
            ):
                recv[head, place, rows(place_in), :] = rotated(ref, gain, norm, cols)

        @pl.when(chunk + ahead < chunks)
        def _():
            for index in range(CHUNK):
                send_values((chunk + ahead) * CHUNK + index)

    @pl.loop(0, min(SENT_AHEAD, chunks))
    def _(chunk):
        send_pair(chunk)

    bounds = []
    running = len_ref[0, 0]
    for clip in range(clips):
        bounds.append(running)
        if clip + 1 < clips:
            running = running + len_ref[0, clip + 1]

    def straddle(middle):
        first, last = jnp.int32(0), jnp.int32(n * tok)
        for bound in bounds:
            first = jnp.maximum(first, jnp.where(bound <= middle, bound, 0))
            last = jnp.minimum(last, jnp.where(bound > middle, bound, n * tok))
        below, above = middle - first, last - middle
        mode = jnp.int32(len(plan.modes) - 1)
        for number in reversed(range(len(plan.modes) - 1)):
            count, up, down = plan.modes[number]
            fits = below <= up * TILE
            if count < heads:
                fits = fits & (above <= down * TILE)
            mode = jnp.where(fits, number, mode)
        return first, last, mode

    token_start = side * group_tokens
    straddles = straddle(token_start), straddle(token_start + group_tokens)

    def clear(begin, end):
        @pl.loop(0, heads)
        def _(head):
            recv[head, :, begin:end, :] = jnp.zeros((4, end - begin, HEAD_DIM), jnp.bfloat16)

    clear(2 * group_tokens, plan.span)

    @pl.when(side == 0)
    def _():
        clear(0, group_tokens)

    def segment(shape, dim, start, shift):
        inside = lax.broadcasted_iota(jnp.int32, shape, dim) + start
        places = inside + (token_start - shift)
        found = jnp.zeros(shape, jnp.int32)
        for bound in bounds:
            found = found + (places >= bound).astype(jnp.int32)
        valid = (inside < window) & (places >= 0) & (places < n * tok)
        return jnp.where(valid, found, -1)

    def masks_of(which):
        held = jnp.full((TILE, HEAD_DIM), straddles[which][2], jnp.int32)
        return [held == mode for mode in range(len(plan.modes))]

    def row_of(upward, mode, tile):
        return (group_tokens if upward else 0) + (tile - (plan.modes[mode][1] if upward else 0)) * TILE

    def select(choices, masks):
        (value, _), *others = choices
        for other, modes in others:
            for mode in modes:
                value = jnp.where(masks[mode], other, value)
        return value

    def gather(target, source, which, upward, region, pair):
        masks = masks_of(which)

        @pl.loop(0, 4)
        def _(place):
            for spot in range(plan.length[pair]):
                wanted = {}
                for mode, sent in enumerate(plan.tables[upward]):
                    if spot < len(sent[pair]):
                        head, tile = sent[pair][spot]
                        wanted.setdefault((head, row_of(upward, mode, tile)), []).append(mode)
                ordered = sorted(wanted.items(), key=lambda item: -len(item[1]))
                choices = [
                    (source[head, place, region + row:region + row + TILE, :], modes)
                    for (head, row), modes in ordered
                ]
                start = (plan.begin[pair] + spot) * TILE
                target[which, place, start:start + TILE, :] = select(choices, masks)

    def scatter(source, target, which, upward, region, pair, merged):
        masks = masks_of(which)
        first, last, mode_now = straddles[which]
        lane_rows = lax.broadcasted_iota(jnp.int32, (TILE, HEAD_DIM), 0)
        limits = []
        for mode in range(len(plan.modes)):
            if upward:
                limits.append(jnp.where(mode_now == mode, first, n * tok))
            else:
                limits.append(jnp.where(mode_now == mode, last, -1))

        @pl.loop(0, 4)
        def _(place):
            for head in range(pair * plan.width, (pair + 1) * plan.width):
                wanted = {}
                for mode, (_, up, down) in enumerate(plan.modes):
                    for tile in range(up if upward else down):
                        spot = plan.spot.get((upward, mode, head, tile))
                        if spot is not None:
                            row = row_of(upward, mode, tile)
                            wanted.setdefault(row, {}).setdefault(spot, []).append(mode)
                for row, spots in wanted.items():
                    ordered = sorted(spots.items(), key=lambda item: -len(item[1]))
                    choices = [
                        (source[which, place, spot * TILE:(spot + 1) * TILE, :], modes)
                        for spot, modes in ordered
                    ]
                    here = region + row
                    if merged:
                        tokens = lane_rows + (token_start + row)
                        inside = [tokens >= limit if upward else tokens < limit for limit in limits]
                        own = target[head, place, here:here + TILE, :]
                        value = select([(own, [])] + choices, inside)
                    else:
                        value = select(choices, masks)
                    target[head, place, here:here + TILE, :] = value

    def part_of(ref, which, pair):
        return ref.at[which, :, pl.ds(plan.begin[pair] * TILE, plan.length[pair] * TILE), :]

    def wait_messages(ref, sem, which, upward, pair):
        begin = plan.until[upward][pair - 1] + 1 if pair else 0
        for number in range(begin, plan.until[upward][pair] + 1):
            held = part_of(ref, which, number)
            pltpu.make_async_copy(held, held, sem.at[which, number]).wait()

    def relay(pair):
        for head in range(pair * plan.width, (pair + 1) * plan.width):
            arrived = recv.at[head, :, pl.ds(0, (members - 1) * tok), :]
            pltpu.make_async_copy(arrived, arrived, in_recv.at[head]).wait()
            own = recv.at[head, pl.ds(2, 2), pl.ds(0, tok), :]
            pltpu.make_async_copy(own, own, own_sem.at[head]).wait()

        def act(which, group):
            gather(give, recv, which, which == 1, group_tokens, pair)
            remote(
                part_of(give, which, pair), part_of(take, 1 - which, pair),
                halo_send.at[which], halo_recv.at[1 - which, pair], device(group, place_in),
            ).start()

        each_side(act)

    def arrive(pair):
        def act(which, group):
            upward = which == 0
            wait_messages(take, halo_recv, which, upward, pair)
            scatter(take, recv, which, upward, 0 if upward else 2 * group_tokens, pair, False)

        each_side(act)

    def attend(chunk):
        @pl.loop(0, CHUNK)
        def _(index):
            head = chunk * CHUNK + index
            shift = jnp.int32(plan.low[0])
            for other in range(1, heads):
                shift = jnp.where(head == other, plan.low[other], shift)
            attend_head(head, shift)

    def give_results(pair):
        def act(which, group):
            upward = which == 0
            gather(give_back, back, which, upward, 0 if upward else 2 * group_tokens, pair)
            remote(
                part_of(give_back, which, pair), part_of(take_back, 1 - which, pair),
                beside_send.at[which], beside_recv.at[1 - which, pair],
                device(group, place_in),
            ).start()

        each_side(act)

    def attend_head(head, shift):
        base = group_tokens - shift

        def at(start, size):
            return pl.ds(pl.multiple_of(base + start, TILE), size)

        whole = window * padded <= WHOLE_SCORES
        step_rows = window if whole else QUERY_BLOCK
        if not whole:
            key_acc[...] = jnp.zeros_like(key_acc)
            value_acc[...] = jnp.zeros_like(value_acc)
        for start in range(0, window, step_rows):
            block = min(step_rows, window - start)
            first = max(0, start - reach) // LANES * LANES
            last = min(padded, -(-(start + block + reach) // LANES) * LANES)
            query = recv[head, 0, at(start, block), :]
            keys = recv[head, 1, at(first, last - first), :]
            value_rows = recv[head, 2, at(first, last - first), :]
            cot = recv[head, 3, at(start, block), :]
            live = segment((block, 1), 0, start, shift) == segment((1, last - first), 1, first, shift)
            scores = jnp.where(live, dot(query, keys, 1, 1), -1e30)
            highest = jnp.max(scores, axis=1, keepdims=True)
            expon = jnp.exp2((scores - highest) * (scale * LOG2_E))
            probs = expon * (1.0 / jnp.sum(expon, axis=1, keepdims=True))
            half = probs.astype(jnp.bfloat16)
            context = dot(half, value_rows, 1, 0).astype(jnp.bfloat16)
            delta = jnp.sum(
                cot.astype(jnp.float32) * context.astype(jnp.float32), axis=1, keepdims=True
            )
            dprob = dot(cot, value_rows, 1, 1)
            dscore = (probs * (dprob - delta)).astype(jnp.bfloat16)
            back[head, 2, at(start, block), :] = context
            back[head, 0, at(start, block), :] = (dot(dscore, keys, 1, 0) * scale).astype(jnp.bfloat16)
            key_part = (dot(query, dscore, 0, 0) * scale).T
            value_part = dot(cot, half, 0, 0).T
            if whole:
                back[head, 1, at(0, window), :] = key_part[0:window].astype(jnp.bfloat16)
                back[head, 3, at(0, window), :] = value_part[0:window].astype(jnp.bfloat16)
            else:
                key_acc[first:last, :] += key_part
                value_acc[first:last, :] += value_part
        if not whole:
            back[head, 1, at(0, window), :] = key_acc[0:window, :].astype(jnp.bfloat16)
            back[head, 3, at(0, window), :] = value_acc[0:window, :].astype(jnp.bfloat16)

    def merge(pair):
        def act(which, group):
            upward = which == 1
            wait_messages(take_back, beside_recv, which, upward, pair)
            scatter(take_back, back, which, upward, group_tokens, pair, True)

        each_side(act)

    def distribute(chunk):
        outward(chunk, 0, (dq_ref, dk_ref), out_send, out_recv, True)

        @pl.when(chunk < chunks - DEFERRED)
        def _():
            outward(chunk, 2, (att_ref, dv_ref), late_send, late_recv, False)

    def outward(chunk, first, targets, send, receive, each):
        for index in range(CHUNK):
            head = chunk * CHUNK + index
            cols = columns(place_in, head)

            @pl.loop(1, members)
            def _(step):
                other = member(step)
                for place, target in enumerate(targets):
                    remote(
                        back.at[head, first + place, rows(other), :], target.at[:, cols],
                        send.at[0], receive.at[head if each else 0], device(side, other),
                    ).start()

            for place, target in enumerate(targets):
                target[:, cols] = back[head, first + place, rows(place_in), :]

    def arrived_pair(head, sem):
        held = recv.at[head, 0:2, pl.ds(0, (members - 1) * tok), :]
        pltpu.make_async_copy(held, held, sem.at[head]).wait()

    def turned_back(grad, ref, norm, cols):
        grads = grad[:, cols].astype(jnp.float32)
        turned = grads * cos_ref[...] - pltpu.roll(grads, HEAD_DIM // 2, 1) * sin_ref[...]
        return turned, ref[:, cols].astype(jnp.float32) * norm[...]

    sides = (
        (dq_ref, q_ref, gq_ref, scale_q, inner_q), (dk_ref, k_ref, gk_ref, scale_k, inner_k),
    )
    inner_q[...] = zero
    inner_k[...] = zero

    def first_pass(chunk):
        for index in range(CHUNK):
            head = chunk * CHUNK + index
            arrived_pair(head, out_recv)

            @pl.loop(0, members)
            def _(owner):
                cols = columns(owner, head)
                for place, (grad, ref, gain, norm, inner) in enumerate(sides):
                    turned, hat = turned_back(grad, ref, norm, cols)
                    both = turned * hat
                    row = place * shared + lax.rem(head, shared)
                    part[owner * ratio + head // shared, pl.ds(row, 1), :] = jnp.sum(
                        both, axis=0, keepdims=True
                    )
                    inner[...] += both * gain[:, cols]

    @pl.loop(0, chunks + ATTEND_LAG + DISTRIBUTE_LAG + NORM_LAG)
    def _(step):
        def each_pair(now, act):
            for pair in range(chunks):
                @pl.when(now == pair)
                def _():
                    act(pair)

        each_pair(step, relay)

        @pl.when(step + SENT_AHEAD < chunks)
        def _():
            send_pair(step + SENT_AHEAD)

        attended = step - ATTEND_LAG
        each_pair(attended, arrive)

        @pl.when((attended >= 0) & (attended < chunks))
        def _():
            attend(attended)

        each_pair(attended, give_results)
        merged = attended - DISTRIBUTE_LAG
        each_pair(merged, merge)

        @pl.when((merged >= 0) & (merged < chunks))
        def _():
            distribute(merged)

        @pl.when(step >= ATTEND_LAG + DISTRIBUTE_LAG + NORM_LAG)
        def _():
            first_pass(step - ATTEND_LAG - DISTRIBUTE_LAG - NORM_LAG)

    per = n // replicas

    def portion(index):
        return pl.ds(index * per, per)

    for step in range(1, replicas):
        other = lax.rem(my_dp + step, replicas)
        remote(
            part.at[portion(other)], dp_part.at[my_dp], gain_send.at[0], gain_recv.at[0], (other, me)
        ).start()
    dp_part[my_dp] = part[portion(my_dp)]

    @pl.loop(chunks - min(DEFERRED, chunks), chunks)
    def _(chunk):
        outward(chunk, 2, (att_ref, dv_ref), late_send, late_recv, False)

    means = [
        jnp.broadcast_to(jnp.sum(inner[...], axis=1, keepdims=True) / feature, (tok, LANES))
        for inner in (inner_q, inner_k)
    ]

    def second_pass(index):
        cols = pl.ds(pl.multiple_of(index * LANES, LANES), LANES)
        for (grad, ref, gain, norm, _), mean in zip(sides, means):
            turned, hat = turned_back(grad, ref, norm, cols)
            result = norm[...] * (turned * gain[:, cols] - hat * mean)
            grad[:, cols] = result.astype(jnp.bfloat16)

    pl.loop(0, feature // LANES)(second_pass)

    def wait_all(ref, count, sem):
        held = ref.at[pl.ds(0, count)]
        pltpu.make_async_copy(held, held, sem).wait()

    wait_all(dp_part, replicas - 1, gain_recv.at[0])
    dp_sum[...] = jnp.sum(dp_part[...], axis=0)

    @pl.loop(1, n)
    def _(step):
        other = peer(step)
        remote(
            dp_sum, seq_part.at[me], gain_send.at[1], gain_recv.at[1], (my_dp, other)
        ).start()

    seq_part[me] = dp_sum[...]
    wait_all(seq_part, n - 1, gain_recv.at[1])
    total[...] = jnp.sum(seq_part[...], axis=0) / replicas
    for step in range(1, replicas):
        other = lax.rem(my_dp + step, replicas)
        remote(
            total, gain_ref.at[portion(my_dp)], gain_send.at[2], gain_recv.at[2], (other, me)
        ).start()
    gain_ref[portion(my_dp)] = total[...]
    wait_all(dp_part, replicas - 1, gain_recv.at[2])

    wait_all(dp_part, replicas - 1, gain_send.at[0])
    wait_all(seq_part, n - 1, gain_send.at[1])
    wait_all(dp_part, replicas - 1, gain_send.at[2])

    moved = recv.at[:, :, pl.ds(0, (members - 1) * tok), :]
    pltpu.make_async_copy(moved, moved, in_send.at[0]).wait()
    halves = recv.at[:, 0:2, pl.ds(0, (members - 1) * tok), :]
    for sem in (out_send, late_send, late_recv):
        pltpu.make_async_copy(halves, halves, sem.at[0]).wait()

    def drain(which, group):
        held = give.at[which]
        pltpu.make_async_copy(held, held, halo_send.at[which]).wait()
        pltpu.make_async_copy(held, held, beside_send.at[which]).wait()

    each_side(drain)


def finish(gains_ref, *refs):
    arrays, targets, (gq_ref, gk_ref), sems = refs[:4], refs[4:8], refs[8:10], refs[10]
    copies = [
        pltpu.make_async_copy(source, target, sems.at[index])
        for index, (source, target) in enumerate(zip(arrays, targets))
    ]
    for copy in copies:
        copy.start()
    owners, shared = gains_ref.shape[0], gains_ref.shape[1] // 2
    for owner in range(owners):
        for row in range(shared):
            cols = slice((owner * shared + row) * LANES, (owner * shared + row + 1) * LANES)
            gq_ref[:, cols] = gains_ref[owner, row:row + 1, :]
            gk_ref[:, cols] = gains_ref[owner, shared + row:shared + row + 1, :]
    for copy in copies:
        copy.wait()


def on_device(q_raw, k_raw, values, grad_out, q_gain, k_gain, lengths, positions):
    n = lax.axis_size("seq")
    replicas = lax.axis_size("dp")
    tok, feature = q_raw.shape[1:]
    shared = feature // n // HEAD_DIM
    heads = GROUPS * shared
    tokens = n * tok
    reach = tokens // 3 - 1
    group_tokens = tokens // GROUPS
    chunks = heads // CHUNK
    plan = Plan(reach + 1, group_tokens, heads, chunks)
    sizes = (n, replicas, heads, tok, lengths.shape[1], reach, plan)
    vmem = pl.BlockSpec(memory_space=pltpu.VMEM)
    hbm = pl.BlockSpec(memory_space=pl.ANY)
    gain_rows = (2 * shared, LANES)
    half, full = jnp.bfloat16, jnp.float32
    *outs, gains = pl.pallas_call(
        functools.partial(kernel, sizes),
        out_shape=(
            *[pltpu.VMEM((tok, feature), half)] * 4,
            pltpu.VMEM((n,) + gain_rows, full),
        ),
        in_specs=[
            pl.BlockSpec(memory_space=pltpu.SMEM), hbm, hbm, hbm, hbm, vmem, vmem, vmem, vmem,
        ],
        out_specs=(vmem,) * 5,
        scratch_shapes=[
            pltpu.VMEM((tok, feature), half),
            pltpu.VMEM((tok, feature), half),
            pltpu.VMEM((tok, HEAD_DIM), full),
            pltpu.VMEM((tok, HEAD_DIM), full),
            pltpu.VMEM((tok, LANES), full),
            pltpu.VMEM((tok, LANES), full),
            pltpu.VMEM((2, 4, plan.tiles * TILE, HEAD_DIM), half),
            pltpu.VMEM((2, 4, plan.tiles * TILE, HEAD_DIM), half),
            pltpu.VMEM((2, 4, plan.tiles * TILE, HEAD_DIM), half),
            pltpu.VMEM((2, 4, plan.tiles * TILE, HEAD_DIM), half),
            pltpu.VMEM((heads, n // GROUPS, 2, tok, HEAD_DIM), half),
            pltpu.VMEM((heads, 4, plan.span, HEAD_DIM), half),
            pltpu.VMEM((heads, 4, plan.span, HEAD_DIM), half),
            pltpu.VMEM((plan.padded, HEAD_DIM), full),
            pltpu.VMEM((plan.padded, HEAD_DIM), full),
            pltpu.VMEM((tok, LANES), full),
            pltpu.VMEM((tok, LANES), full),
            pltpu.VMEM((n,) + gain_rows, full),
            pltpu.VMEM((n, n // replicas) + gain_rows, full),
            pltpu.VMEM((n // replicas,) + gain_rows, full),
            pltpu.VMEM((replicas, n // replicas) + gain_rows, full),
            pltpu.VMEM((n // replicas,) + gain_rows, full),
            pltpu.SemaphoreType.DMA((2,)),
            pltpu.SemaphoreType.DMA((1,)),
            pltpu.SemaphoreType.DMA((heads,)),
            pltpu.SemaphoreType.DMA((heads,)),
            pltpu.SemaphoreType.DMA((1,)),
            pltpu.SemaphoreType.DMA((heads,)),
            pltpu.SemaphoreType.DMA((1,)),
            pltpu.SemaphoreType.DMA((1,)),
            pltpu.SemaphoreType.DMA((3,)),
            pltpu.SemaphoreType.DMA((3,)),
            pltpu.SemaphoreType.DMA((2,)),
            pltpu.SemaphoreType.DMA((2, chunks)),
            pltpu.SemaphoreType.DMA((2,)),
            pltpu.SemaphoreType.DMA((2, chunks)),
        ],
        compiler_params=pltpu.CompilerParams(
            collective_id=0, has_side_effects=True, vmem_limit_bytes=56 * 1024 * 1024
        ),
    )(
        lengths, q_raw[0], k_raw[0], values[0], grad_out[0],
        q_gain[None], k_gain[None], positions[0][:, None], jnp.asarray(rope_constants(HEAD_DIM)),
    )
    attended, grad_q, grad_k, grad_v, gain_q, gain_k = pl.pallas_call(
        finish,
        out_shape=(jax.ShapeDtypeStruct((tok, feature), half),) * 4
        + (jax.ShapeDtypeStruct((1, feature), full),) * 2,
        in_specs=[vmem] * 5,
        out_specs=(hbm,) * 4 + (vmem,) * 2,
        scratch_shapes=[pltpu.SemaphoreType.DMA((4,))],
        compiler_params=pltpu.CompilerParams(vmem_limit_bytes=6 * 1024 * 1024),
    )(gains, *outs)
    return (
        attended[None], grad_q[None], grad_k[None], grad_v[None], gain_q[0], gain_k[0],
    )


def solution(mesh):
    tokens = P("dp", "seq", None)
    return jax.shard_map(
        on_device,
        mesh=mesh,
        in_specs=(tokens, tokens, tokens, tokens, P(), P(), P("dp", None), P("dp", None, "seq")),
        out_specs=(tokens, tokens, tokens, tokens, P(), P()),
        check_vma=False,
    )
```

```python
import functools
import random

import jax
import jax.numpy as jnp
import numpy as np
from jax import lax
from jax.experimental import pallas as pl
from jax.experimental.pallas import tpu as pltpu
from jax.sharding import PartitionSpec as P

HEAD_DIM = 128
LANES = 128
QUERY_BLOCK = 256
WHOLE_SCORES = 1 << 19
LOG2_E = float(np.log2(np.e))
GROUPS = 4
CHUNK = 2
TILE = 16
ATTEND_LAG = 2
DISTRIBUTE_LAG = 2
NORM_LAG = 1
DEFERRED = 2
AHEAD = 1
SENT_AHEAD = 8
EPSILON = 1e-06
MESH = pl.DeviceIdType.MESH


def rope_constants(head_dim):
    half = head_dim // 2
    sixth = head_dim // 6
    first = half - 2 * sixth
    pairs = np.arange(head_dim) % half
    section = (pairs >= first).astype(np.int32) + (pairs >= first + sixth).astype(np.int32)
    begin = np.where(section == 0, 0, np.where(section == 1, first, first + sixth))
    number = np.where(section == 0, first, sixth)
    freqs = (10000.0 ** (-(pairs - begin) / number)).astype(np.float32)
    return (section == np.arange(3)[:, None]).astype(np.float32) * freqs


def needed_modes(longest, rows, heads):
    own = rows // TILE
    total = heads
    while True:
        size = {n: min(own, total // n) for n in range(1, heads + 1)}
        modes, below = [(heads, size[heads], 0)], size[heads] * TILE + 1
        while below <= rows and longest - below > size[heads] * TILE:
            found = [
                (size[n], n) for n in range(1, heads) if size[heads - n] * TILE >= longest - below
            ]
            if not found or max(found)[0] * TILE < below:
                break
            up, count = max(found)
            modes.append((count, up, size[heads - count]))
            below = up * TILE + 1
        else:
            if longest - rows - 1 <= size[heads] * TILE:
                return total, modes + [(0, 0, size[heads])]
        total += 1


def messages(ranks, modes, pairs, base):
    width = len(ranks) // pairs
    tables = {True: [], False: []}
    for upward in tables:
        for count, up, down in modes:
            queue, sent = [], []
            for pair in range(pairs):
                for head in range(pair * width, (pair + 1) * width):
                    if (ranks[head] < count) == upward:
                        queue += [(head, tile) for tile in range(up if upward else down)]
                room = base if pair < pairs - 1 else len(queue)
                sent.append(queue[:room])
                queue = queue[room:]
            tables[upward].append(sent)
    return tables


def ranked(modes, heads, pairs, base):
    rng = random.Random(0)
    width = heads // pairs

    def cost(ranks):
        worst = late = 0
        for count, up, down in modes:
            for upward, size in ((True, up), (False, down)):
                left = 0
                for pair in range(pairs):
                    held = ranks[pair * width:(pair + 1) * width]
                    left += size * sum((rank < count) == upward for rank in held)
                    if pair < pairs - 1:
                        left = max(0, left - base)
                        late += left
                worst = max(worst, left)
        return worst, late

    best = None
    for _ in range(20):
        ranks = list(range(heads))
        rng.shuffle(ranks)
        now, stall = cost(ranks), 0
        while stall < 150:
            i, j = rng.randrange(heads), rng.randrange(heads)
            ranks[i], ranks[j] = ranks[j], ranks[i]
            new = cost(ranks)
            if new <= now:
                stall = 0 if new < now else stall + 1
                now = new
            else:
                ranks[i], ranks[j] = ranks[j], ranks[i]
                stall += 1
        if best is None or now < best[0]:
            best = (now, list(ranks))
    return best[1]


class Plan:
    def __init__(self, longest, rows, heads, pairs):
        self.pairs, self.width = pairs, heads // pairs
        total, self.modes = needed_modes(longest, rows, heads)
        base = -(-total // pairs)
        ranks = ranked(self.modes, heads, pairs, base)
        self.tables = messages(ranks, self.modes, pairs, base)
        last = max(len(sent[-1]) for sents in self.tables.values() for sent in sents)
        self.length = [base] * (pairs - 1) + [last]
        self.begin = [base * pair for pair in range(pairs)]
        self.tiles = base * (pairs - 1) + last
        self.spot, self.until = {}, {}
        for upward, sents in self.tables.items():
            self.until[upward] = [0] * pairs
            for mode, sent in enumerate(sents):
                for number, tiles in enumerate(sent):
                    for place, (head, tile) in enumerate(tiles):
                        self.spot[upward, mode, head, tile] = self.begin[number] + place
                        pair = head // self.width
                        self.until[upward][pair] = max(self.until[upward][pair], number)
            for pair in range(1, pairs):
                self.until[upward][pair] = max(self.until[upward][pair - 1:pair + 1])
            self.until[upward][-1] = pairs - 1
        self.low = [max(up for count, up, _ in self.modes if rank < count) * TILE for rank in ranks]
        self.high = [max(dn for count, _, dn in self.modes if rank >= count) * TILE for rank in ranks]
        self.window = rows + max(low + high for low, high in zip(self.low, self.high))
        self.padded = -(-self.window // LANES) * LANES
        self.span = max(3 * rows, rows - min(self.low) + self.padded)


def dot(left, right, left_dim, right_dim):
    return lax.dot_general(
        left, right, (((left_dim,), (right_dim,)), ((), ())), preferred_element_type=jnp.float32
    )


def kernel(
    sizes,
    len_ref, q_hbm, k_hbm, v_ref, do_ref, gq_ref, gk_ref, pos_ref, freq_ref,
    att_ref, dq_ref, dk_ref, dv_ref, gain_ref,
    q_ref, k_ref, cos_ref, sin_ref, inner_q, inner_k,
    give, take, give_back, take_back, sent, recv, back, key_acc, value_acc, scale_q, scale_k,
    part, seq_part, dp_sum, dp_part, total,
    raw_sem, in_send, in_recv, own_sem, out_send, out_recv, late_send, late_recv,
    gain_send, gain_recv,
    halo_send, halo_recv, beside_send, beside_recv,
):
    n, replicas, heads, tok, clips, reach, plan = sizes
    members = n // GROUPS
    group_tokens = members * tok
    chunks = heads // CHUNK
    window, padded = plan.window, plan.padded
    feature = members * heads * HEAD_DIM
    ratio = GROUPS
    shared = heads // ratio
    me = lax.axis_index("seq")
    side = me // members
    place_in = lax.rem(me, members)
    my_dp = lax.axis_index("dp")
    scale = HEAD_DIM ** (-0.5)

    def peer(step):
        return lax.rem(me + step, n)

    def member(step):
        return lax.rem(place_in + step, members)

    def device(group, index):
        return (my_dp, group * members + index)

    def columns(owner, head):
        return pl.ds(pl.multiple_of((owner * heads + head) * HEAD_DIM, HEAD_DIM), HEAD_DIM)

    def rows(owner):
        return pl.ds(pl.multiple_of(group_tokens + owner * tok, TILE), tok)

    def each_side(act):
        @pl.when(side > 0)
        def _():
            act(0, side - 1)

        @pl.when(side < GROUPS - 1)
        def _():
            act(1, side + 1)

    def remote(src, dst, send_sem, recv_sem, device):
        return pltpu.make_async_remote_copy(
            src_ref=src, dst_ref=dst, send_sem=send_sem, recv_sem=recv_sem,
            device_id=device, device_id_type=MESH,
        )

    loads = [
        pltpu.make_async_copy(q_hbm, q_ref, raw_sem.at[0]),
        pltpu.make_async_copy(k_hbm, k_ref, raw_sem.at[1]),
    ]
    for load in loads:
        load.start()

    barrier = pltpu.get_barrier_semaphore()

    def greet(target):
        pl.semaphore_signal(barrier, inc=1, device_id=target, device_id_type=MESH)

    for step in range(1, members):
        greet(device(side, member(step)))
    for step in range(1, replicas):
        greet((lax.rem(my_dp + step, replicas), me))
    each_side(lambda which, group: greet(device(group, place_in)))
    sides_here = jnp.minimum(side, 1) + jnp.minimum(GROUPS - 1 - side, 1)
    pl.semaphore_wait(barrier, members - 1 + replicas - 1 + sides_here)

    def send_values(head):
        cols = columns(place_in, head)
        for place, ref in ((2, v_ref), (3, do_ref)):
            pltpu.make_async_copy(
                ref.at[:, cols], recv.at[head, place, rows(place_in), :], own_sem.at[head]
            ).start()

        @pl.loop(1, members)
        def _(step):
            other = member(step)
            for place, ref in ((2, v_ref), (3, do_ref)):
                remote(
                    ref.at[:, columns(other, head)], recv.at[head, place, rows(place_in), :],
                    in_send.at[0], in_recv.at[head], device(side, other),
                ).start()

    ahead = min(AHEAD, chunks)
    for head in range(ahead * CHUNK):
        send_values(head)

    held = jnp.concatenate([pos_ref[axis] for axis in range(3)], axis=0)
    angle = lax.dot_general(
        held.astype(jnp.float32), freq_ref[...], (((0,), (0,)), ((), ())),
        precision=lax.Precision.HIGHEST, preferred_element_type=jnp.float32,
    )
    negative = lax.broadcasted_iota(jnp.int32, (tok, HEAD_DIM), 1) < HEAD_DIM // 2
    cos_ref[...] = jnp.cos(angle)
    sine = jnp.sin(angle)
    sin_ref[...] = jnp.where(negative, -sine, sine)
    for load in loads:
        load.wait()

    def squares(index, sums):
        cols = pl.ds(pl.multiple_of(index * LANES, LANES), LANES)
        query = q_ref[:, cols].astype(jnp.float32)
        keys = k_ref[:, cols].astype(jnp.float32)
        return sums[0] + query * query, sums[1] + keys * keys

    zero = jnp.zeros((tok, LANES), jnp.float32)
    sum_q, sum_k = lax.fori_loop(0, feature // LANES, squares, (zero, zero))
    for sums, target in ((sum_q, scale_q), (sum_k, scale_k)):
        mean = jnp.sum(sums, axis=1, keepdims=True) / feature
        target[...] = jnp.broadcast_to(lax.rsqrt(mean + EPSILON), (tok, LANES))

    def rotated(ref, gain, norm, cols):
        x = ref[:, cols].astype(jnp.float32) * norm[...] * gain[:, cols]
        turned = x * cos_ref[...] + pltpu.roll(x, HEAD_DIM // 2, 1) * sin_ref[...]
        return turned.astype(jnp.bfloat16)

    def send_pair(chunk):
        for index in range(CHUNK):
            head = chunk * CHUNK + index

            @pl.loop(1, members)
            def _(step):
                other = member(step)
                cols = columns(other, head)
                sent[head, other, 0] = rotated(q_ref, gq_ref, scale_q, cols)
                sent[head, other, 1] = rotated(k_ref, gk_ref, scale_k, cols)
                remote(
                    sent.at[head, other], recv.at[head, 0:2, rows(place_in), :],
                    in_send.at[0], in_recv.at[head], device(side, other),
                ).start()

            cols = columns(place_in, head)
            for place, (ref, gain, norm) in enumerate(
                ((q_ref, gq_ref, scale_q), (k_ref, gk_ref, scale_k))
            ):
                recv[head, place, rows(place_in), :] = rotated(ref, gain, norm, cols)

        @pl.when(chunk + ahead < chunks)
        def _():
            for index in range(CHUNK):
                send_values((chunk + ahead) * CHUNK + index)

    @pl.loop(0, min(SENT_AHEAD, chunks))
    def _(chunk):
        send_pair(chunk)

    bounds = []
    running = len_ref[0, 0]
    for clip in range(clips):
        bounds.append(running)
        if clip + 1 < clips:
            running = running + len_ref[0, clip + 1]

    def straddle(middle):
        first, last = jnp.int32(0), jnp.int32(n * tok)
        for bound in bounds:
            first = jnp.maximum(first, jnp.where(bound <= middle, bound, 0))
            last = jnp.minimum(last, jnp.where(bound > middle, bound, n * tok))
        below, above = middle - first, last - middle
        mode = jnp.int32(len(plan.modes) - 1)
        for number in reversed(range(len(plan.modes) - 1)):
            count, up, down = plan.modes[number]
            fits = below <= up * TILE
            if count < heads:
                fits = fits & (above <= down * TILE)
            mode = jnp.where(fits, number, mode)
        return first, last, mode

    token_start = side * group_tokens
    straddles = straddle(token_start), straddle(token_start + group_tokens)

    def clear(begin, end):
        @pl.loop(0, heads)
        def _(head):
            recv[head, :, begin:end, :] = jnp.zeros((4, end - begin, HEAD_DIM), jnp.bfloat16)

    clear(2 * group_tokens, plan.span)

    @pl.when(side == 0)
    def _():
        clear(0, group_tokens)

    def segment(shape, dim, start, shift):
        inside = lax.broadcasted_iota(jnp.int32, shape, dim) + start
        places = inside + (token_start - shift)
        found = jnp.zeros(shape, jnp.int32)
        for bound in bounds:
            found = found + (places >= bound).astype(jnp.int32)
        valid = (inside < window) & (places >= 0) & (places < n * tok)
        return jnp.where(valid, found, -1)

    def masks_of(which):
        held = jnp.full((TILE, HEAD_DIM), straddles[which][2], jnp.int32)
        return [held == mode for mode in range(len(plan.modes))]

    def row_of(upward, mode, tile):
        return (group_tokens if upward else 0) + (tile - (plan.modes[mode][1] if upward else 0)) * TILE

    def select(choices, masks):
        (value, _), *others = choices
        for other, modes in others:
            for mode in modes:
                value = jnp.where(masks[mode], other, value)
        return value

    def gather(target, source, which, upward, region, pair):
        masks = masks_of(which)

        @pl.loop(0, 4)
        def _(place):
            for spot in range(plan.length[pair]):
                wanted = {}
                for mode, sent in enumerate(plan.tables[upward]):
                    if spot < len(sent[pair]):
                        head, tile = sent[pair][spot]
                        wanted.setdefault((head, row_of(upward, mode, tile)), []).append(mode)
                ordered = sorted(wanted.items(), key=lambda item: -len(item[1]))
                choices = [
                    (source[head, place, region + row:region + row + TILE, :], modes)
                    for (head, row), modes in ordered
                ]
                start = (plan.begin[pair] + spot) * TILE
                target[which, place, start:start + TILE, :] = select(choices, masks)

    def scatter(source, target, which, upward, region, pair, merged):
        masks = masks_of(which)
        first, last, mode_now = straddles[which]
        lane_rows = lax.broadcasted_iota(jnp.int32, (TILE, HEAD_DIM), 0)
        limits = []
        for mode in range(len(plan.modes)):
            if upward:
                limits.append(jnp.where(mode_now == mode, first, n * tok))
            else:
                limits.append(jnp.where(mode_now == mode, last, -1))

        @pl.loop(0, 4)
        def _(place):
            for head in range(pair * plan.width, (pair + 1) * plan.width):
                wanted = {}
                for mode, (_, up, down) in enumerate(plan.modes):
                    for tile in range(up if upward else down):
                        spot = plan.spot.get((upward, mode, head, tile))
                        if spot is not None:
                            row = row_of(upward, mode, tile)
                            wanted.setdefault(row, {}).setdefault(spot, []).append(mode)
                for row, spots in wanted.items():
                    ordered = sorted(spots.items(), key=lambda item: -len(item[1]))
                    choices = [
                        (source[which, place, spot * TILE:(spot + 1) * TILE, :], modes)
                        for spot, modes in ordered
                    ]
                    here = region + row
                    if merged:
                        tokens = lane_rows + (token_start + row)
                        inside = [tokens >= limit if upward else tokens < limit for limit in limits]
                        own = target[head, place, here:here + TILE, :]
                        value = select([(own, [])] + choices, inside)
                    else:
                        value = select(choices, masks)
                    target[head, place, here:here + TILE, :] = value

    def part_of(ref, which, pair):
        return ref.at[which, :, pl.ds(plan.begin[pair] * TILE, plan.length[pair] * TILE), :]

    def wait_messages(ref, sem, which, upward, pair):
        begin = plan.until[upward][pair - 1] + 1 if pair else 0
        for number in range(begin, plan.until[upward][pair] + 1):
            held = part_of(ref, which, number)
            pltpu.make_async_copy(held, held, sem.at[which, number]).wait()

    def relay(pair):
        for head in range(pair * plan.width, (pair + 1) * plan.width):
            arrived = recv.at[head, :, pl.ds(0, (members - 1) * tok), :]
            pltpu.make_async_copy(arrived, arrived, in_recv.at[head]).wait()
            own = recv.at[head, pl.ds(2, 2), pl.ds(0, tok), :]
            pltpu.make_async_copy(own, own, own_sem.at[head]).wait()

        def act(which, group):
            gather(give, recv, which, which == 1, group_tokens, pair)
            remote(
                part_of(give, which, pair), part_of(take, 1 - which, pair),
                halo_send.at[which], halo_recv.at[1 - which, pair], device(group, place_in),
            ).start()

        each_side(act)

    def arrive(pair):
        def act(which, group):
            upward = which == 0
            wait_messages(take, halo_recv, which, upward, pair)
            scatter(take, recv, which, upward, 0 if upward else 2 * group_tokens, pair, False)

        each_side(act)

    def attend(chunk):
        @pl.loop(0, CHUNK)
        def _(index):
            head = chunk * CHUNK + index
            shift = jnp.int32(plan.low[0])
            for other in range(1, heads):
                shift = jnp.where(head == other, plan.low[other], shift)
            attend_head(head, shift)

    def give_results(pair):
        def act(which, group):
            upward = which == 0
            gather(give_back, back, which, upward, 0 if upward else 2 * group_tokens, pair)
            remote(
                part_of(give_back, which, pair), part_of(take_back, 1 - which, pair),
                beside_send.at[which], beside_recv.at[1 - which, pair],
                device(group, place_in),
            ).start()

        each_side(act)

    def attend_head(head, shift):
        base = group_tokens - shift

        def at(start, size):
            return pl.ds(pl.multiple_of(base + start, TILE), size)

        whole = window * padded <= WHOLE_SCORES
        step_rows = window if whole else QUERY_BLOCK
        if not whole:
            key_acc[...] = jnp.zeros_like(key_acc)
            value_acc[...] = jnp.zeros_like(value_acc)
        for start in range(0, window, step_rows):
            block = min(step_rows, window - start)
            first = max(0, start - reach) // LANES * LANES
            last = min(padded, -(-(start + block + reach) // LANES) * LANES)
            query = recv[head, 0, at(start, block), :]
            keys = recv[head, 1, at(first, last - first), :]
            value_rows = recv[head, 2, at(first, last - first), :]
            cot = recv[head, 3, at(start, block), :]
            live = segment((block, 1), 0, start, shift) == segment((1, last - first), 1, first, shift)
            scores = jnp.where(live, dot(query, keys, 1, 1), -1e30)
            highest = jnp.max(scores, axis=1, keepdims=True)
            expon = jnp.exp2((scores - highest) * (scale * LOG2_E))
            probs = expon * (1.0 / jnp.sum(expon, axis=1, keepdims=True))
            half = probs.astype(jnp.bfloat16)
            context = dot(half, value_rows, 1, 0).astype(jnp.bfloat16)
            delta = jnp.sum(
                cot.astype(jnp.float32) * context.astype(jnp.float32), axis=1, keepdims=True
            )
            dprob = dot(cot, value_rows, 1, 1)
            dscore = (probs * (dprob - delta)).astype(jnp.bfloat16)
            back[head, 2, at(start, block), :] = context
            back[head, 0, at(start, block), :] = (dot(dscore, keys, 1, 0) * scale).astype(jnp.bfloat16)
            key_part = (dot(query, dscore, 0, 0) * scale).T
            value_part = dot(cot, half, 0, 0).T
            if whole:
                back[head, 1, at(0, window), :] = key_part[0:window].astype(jnp.bfloat16)
                back[head, 3, at(0, window), :] = value_part[0:window].astype(jnp.bfloat16)
            else:
                key_acc[first:last, :] += key_part
                value_acc[first:last, :] += value_part
        if not whole:
            back[head, 1, at(0, window), :] = key_acc[0:window, :].astype(jnp.bfloat16)
            back[head, 3, at(0, window), :] = value_acc[0:window, :].astype(jnp.bfloat16)

    def merge(pair):
        def act(which, group):
            upward = which == 1
            wait_messages(take_back, beside_recv, which, upward, pair)
            scatter(take_back, back, which, upward, group_tokens, pair, True)

        each_side(act)

    def distribute(chunk):
        outward(chunk, 0, (dq_ref, dk_ref), out_send, out_recv, True)

        @pl.when(chunk < chunks - DEFERRED)
        def _():
            outward(chunk, 2, (att_ref, dv_ref), late_send, late_recv, False)

    def outward(chunk, first, targets, send, receive, each):
        for index in range(CHUNK):
            head = chunk * CHUNK + index
            cols = columns(place_in, head)

            @pl.loop(1, members)
            def _(step):
                other = member(step)
                for place, target in enumerate(targets):
                    remote(
                        back.at[head, first + place, rows(other), :], target.at[:, cols],
                        send.at[0], receive.at[head if each else 0], device(side, other),
                    ).start()

            for place, target in enumerate(targets):
                target[:, cols] = back[head, first + place, rows(place_in), :]

    def arrived_pair(head, sem):
        held = recv.at[head, 0:2, pl.ds(0, (members - 1) * tok), :]
        pltpu.make_async_copy(held, held, sem.at[head]).wait()

    def turned_back(grad, ref, norm, cols):
        grads = grad[:, cols].astype(jnp.float32)
        turned = grads * cos_ref[...] - pltpu.roll(grads, HEAD_DIM // 2, 1) * sin_ref[...]
        return turned, ref[:, cols].astype(jnp.float32) * norm[...]

    sides = (
        (dq_ref, q_ref, gq_ref, scale_q, inner_q), (dk_ref, k_ref, gk_ref, scale_k, inner_k),
    )
    inner_q[...] = zero
    inner_k[...] = zero

    def first_pass(chunk):
        for index in range(CHUNK):
            head = chunk * CHUNK + index
            arrived_pair(head, out_recv)

            @pl.loop(0, members)
            def _(owner):
                cols = columns(owner, head)
                for place, (grad, ref, gain, norm, inner) in enumerate(sides):
                    turned, hat = turned_back(grad, ref, norm, cols)
                    both = turned * hat
                    row = place * shared + lax.rem(head, shared)
                    part[owner * ratio + head // shared, pl.ds(row, 1), :] = jnp.sum(
                        both, axis=0, keepdims=True
                    )
                    inner[...] += both * gain[:, cols]

    @pl.loop(0, chunks + ATTEND_LAG + DISTRIBUTE_LAG + NORM_LAG)
    def _(step):
        def each_pair(now, act):
            for pair in range(chunks):
                @pl.when(now == pair)
                def _():
                    act(pair)

        each_pair(step, relay)

        @pl.when(step + SENT_AHEAD < chunks)
        def _():
            send_pair(step + SENT_AHEAD)

        attended = step - ATTEND_LAG
        each_pair(attended, arrive)

        @pl.when((attended >= 0) & (attended < chunks))
        def _():
            attend(attended)

        each_pair(attended, give_results)
        merged = attended - DISTRIBUTE_LAG
        each_pair(merged, merge)

        @pl.when((merged >= 0) & (merged < chunks))
        def _():
            distribute(merged)

        @pl.when(step >= ATTEND_LAG + DISTRIBUTE_LAG + NORM_LAG)
        def _():
            first_pass(step - ATTEND_LAG - DISTRIBUTE_LAG - NORM_LAG)

    per = n // replicas

    def portion(index):
        return pl.ds(index * per, per)

    for step in range(1, replicas):
        other = lax.rem(my_dp + step, replicas)
        remote(
            part.at[portion(other)], dp_part.at[my_dp], gain_send.at[0], gain_recv.at[0], (other, me)
        ).start()
    dp_part[my_dp] = part[portion(my_dp)]

    means = [
        jnp.broadcast_to(jnp.sum(inner[...], axis=1, keepdims=True) / feature, (tok, LANES))
        for inner in (inner_q, inner_k)
    ]

    def second_pass(index):
        cols = pl.ds(pl.multiple_of(index * LANES, LANES), LANES)
        for (grad, ref, gain, norm, _), mean in zip(sides, means):
            turned, hat = turned_back(grad, ref, norm, cols)
            result = norm[...] * (turned * gain[:, cols] - hat * mean)
            grad[:, cols] = result.astype(jnp.bfloat16)

    pl.loop(0, feature // LANES)(second_pass)

    def wait_all(ref, count, sem):
        held = ref.at[pl.ds(0, count)]
        pltpu.make_async_copy(held, held, sem).wait()

    wait_all(dp_part, replicas - 1, gain_recv.at[0])
    dp_sum[...] = jnp.sum(dp_part[...], axis=0)

    @pl.loop(1, n)
    def _(step):
        other = peer(step)
        remote(
            dp_sum, seq_part.at[me], gain_send.at[1], gain_recv.at[1], (my_dp, other)
        ).start()

    @pl.loop(chunks - min(DEFERRED, chunks), chunks)
    def _(chunk):
        outward(chunk, 2, (att_ref, dv_ref), late_send, late_recv, False)

    seq_part[me] = dp_sum[...]
    wait_all(seq_part, n - 1, gain_recv.at[1])
    total[...] = jnp.sum(seq_part[...], axis=0) / replicas
    for step in range(1, replicas):
        other = lax.rem(my_dp + step, replicas)
        remote(
            total, gain_ref.at[portion(my_dp)], gain_send.at[2], gain_recv.at[2], (other, me)
        ).start()
    gain_ref[portion(my_dp)] = total[...]
    wait_all(dp_part, replicas - 1, gain_recv.at[2])

    wait_all(dp_part, replicas - 1, gain_send.at[0])
    wait_all(seq_part, n - 1, gain_send.at[1])
    wait_all(dp_part, replicas - 1, gain_send.at[2])

    moved = recv.at[:, :, pl.ds(0, (members - 1) * tok), :]
    pltpu.make_async_copy(moved, moved, in_send.at[0]).wait()
    halves = recv.at[:, 0:2, pl.ds(0, (members - 1) * tok), :]
    for sem in (out_send, late_send, late_recv):
        pltpu.make_async_copy(halves, halves, sem.at[0]).wait()

    def drain(which, group):
        held = give.at[which]
        pltpu.make_async_copy(held, held, halo_send.at[which]).wait()
        pltpu.make_async_copy(held, held, beside_send.at[which]).wait()

    each_side(drain)


def finish(gains_ref, *refs):
    arrays, targets, (gq_ref, gk_ref), sems = refs[:4], refs[4:8], refs[8:10], refs[10]
    copies = [
        pltpu.make_async_copy(source, target, sems.at[index])
        for index, (source, target) in enumerate(zip(arrays, targets))
    ]
    for copy in copies:
        copy.start()
    owners, shared = gains_ref.shape[0], gains_ref.shape[1] // 2
    for owner in range(owners):
        for row in range(shared):
            cols = slice((owner * shared + row) * LANES, (owner * shared + row + 1) * LANES)
            gq_ref[:, cols] = gains_ref[owner, row:row + 1, :]
            gk_ref[:, cols] = gains_ref[owner, shared + row:shared + row + 1, :]
    for copy in copies:
        copy.wait()


def on_device(q_raw, k_raw, values, grad_out, q_gain, k_gain, lengths, positions):
    n = lax.axis_size("seq")
    replicas = lax.axis_size("dp")
    tok, feature = q_raw.shape[1:]
    shared = feature // n // HEAD_DIM
    heads = GROUPS * shared
    tokens = n * tok
    reach = tokens // 3 - 1
    group_tokens = tokens // GROUPS
    chunks = heads // CHUNK
    plan = Plan(reach + 1, group_tokens, heads, chunks)
    sizes = (n, replicas, heads, tok, lengths.shape[1], reach, plan)
    vmem = pl.BlockSpec(memory_space=pltpu.VMEM)
    hbm = pl.BlockSpec(memory_space=pl.ANY)
    gain_rows = (2 * shared, LANES)
    half, full = jnp.bfloat16, jnp.float32
    *outs, gains = pl.pallas_call(
        functools.partial(kernel, sizes),
        out_shape=(
            *[pltpu.VMEM((tok, feature), half)] * 4,
            pltpu.VMEM((n,) + gain_rows, full),
        ),
        in_specs=[
            pl.BlockSpec(memory_space=pltpu.SMEM), hbm, hbm, hbm, hbm, vmem, vmem, vmem, vmem,
        ],
        out_specs=(vmem,) * 5,
        scratch_shapes=[
            pltpu.VMEM((tok, feature), half),
            pltpu.VMEM((tok, feature), half),
            pltpu.VMEM((tok, HEAD_DIM), full),
            pltpu.VMEM((tok, HEAD_DIM), full),
            pltpu.VMEM((tok, LANES), full),
            pltpu.VMEM((tok, LANES), full),
            pltpu.VMEM((2, 4, plan.tiles * TILE, HEAD_DIM), half),
            pltpu.VMEM((2, 4, plan.tiles * TILE, HEAD_DIM), half),
            pltpu.VMEM((2, 4, plan.tiles * TILE, HEAD_DIM), half),
            pltpu.VMEM((2, 4, plan.tiles * TILE, HEAD_DIM), half),
            pltpu.VMEM((heads, n // GROUPS, 2, tok, HEAD_DIM), half),
            pltpu.VMEM((heads, 4, plan.span, HEAD_DIM), half),
            pltpu.VMEM((heads, 4, plan.span, HEAD_DIM), half),
            pltpu.VMEM((plan.padded, HEAD_DIM), full),
            pltpu.VMEM((plan.padded, HEAD_DIM), full),
            pltpu.VMEM((tok, LANES), full),
            pltpu.VMEM((tok, LANES), full),
            pltpu.VMEM((n,) + gain_rows, full),
            pltpu.VMEM((n, n // replicas) + gain_rows, full),
            pltpu.VMEM((n // replicas,) + gain_rows, full),
            pltpu.VMEM((replicas, n // replicas) + gain_rows, full),
            pltpu.VMEM((n // replicas,) + gain_rows, full),
            pltpu.SemaphoreType.DMA((2,)),
            pltpu.SemaphoreType.DMA((1,)),
            pltpu.SemaphoreType.DMA((heads,)),
            pltpu.SemaphoreType.DMA((heads,)),
            pltpu.SemaphoreType.DMA((1,)),
            pltpu.SemaphoreType.DMA((heads,)),
            pltpu.SemaphoreType.DMA((1,)),
            pltpu.SemaphoreType.DMA((1,)),
            pltpu.SemaphoreType.DMA((3,)),
            pltpu.SemaphoreType.DMA((3,)),
            pltpu.SemaphoreType.DMA((2,)),
            pltpu.SemaphoreType.DMA((2, chunks)),
            pltpu.SemaphoreType.DMA((2,)),
            pltpu.SemaphoreType.DMA((2, chunks)),
        ],
        compiler_params=pltpu.CompilerParams(
            collective_id=0, has_side_effects=True, vmem_limit_bytes=56 * 1024 * 1024
        ),
    )(
        lengths, q_raw[0], k_raw[0], values[0], grad_out[0],
        q_gain[None], k_gain[None], positions[0][:, None], jnp.asarray(rope_constants(HEAD_DIM)),
    )
    attended, grad_q, grad_k, grad_v, gain_q, gain_k = pl.pallas_call(
        finish,
        out_shape=(jax.ShapeDtypeStruct((tok, feature), half),) * 4
        + (jax.ShapeDtypeStruct((1, feature), full),) * 2,
        in_specs=[vmem] * 5,
        out_specs=(hbm,) * 4 + (vmem,) * 2,
        scratch_shapes=[pltpu.SemaphoreType.DMA((4,))],
        compiler_params=pltpu.CompilerParams(vmem_limit_bytes=6 * 1024 * 1024),
    )(gains, *outs)
    return (
        attended[None], grad_q[None], grad_k[None], grad_v[None], gain_q[0], gain_k[0],
    )


def solution(mesh):
    tokens = P("dp", "seq", None)
    return jax.shard_map(
        on_device,
        mesh=mesh,
        in_specs=(tokens, tokens, tokens, tokens, P(), P(), P("dp", None), P("dp", None, "seq")),
        out_specs=(tokens, tokens, tokens, tokens, P(), P()),
        check_vma=False,
    )
```
